128 devices in a mesh: row: 16 (over z_lo, y, core), col: 8 (over x, z_hi).
Axes of the slice: x: 4, y: 4, z: 4 (z_hi: 2, z_lo: 2; z = z_hi * 2 + z_lo), core: 2. Of those that a mesh axis runs over, the one named last changes fastest.
Arguments:
- pair: bfloat16 [1024, 1024, 128], P('row', 'col'), may hold values from -6 to 6
- ln_gain: float32 [128], replicated, may hold values from 0.1 to 1.9
- ln_bias: float32 [128], replicated, may hold values from -3 to 3
- gate_weight: bfloat16 [128, 512], replicated, may hold values from -0.5 to 0.5
- up_weight: bfloat16 [128, 512], replicated, may hold values from -0.5 to 0.5
- out_weight: bfloat16 [512, 128], replicated, may hold values from -0.25 to 0.25
- head_weight: bfloat16 [128, 64], replicated, may hold values from -1 to 1
- targets: int32 [1024, 1024], P(('row', 'col')), may hold values from 0 to 63
- pair_mask: int32 [1024, 1024], P(('row', 'col')), may hold values 0 or 1
Outputs:
- pair_out: bfloat16 [1024, 1024, 128], P('row', 'col')
- loss: float32 [], replicated
- grad_gain: float32 [128], replicated
- grad_bias: float32 [128], replicated
- grad_gate: float32 [128, 512], replicated
- grad_up: float32 [128, 512], replicated
- grad_out: float32 [512, 128], replicated
- grad_head: float32 [128, 64], replicated
The draws below stay inside these ranges and needn't reach their ends.
All inputs are finite; a program needn't handle non-finite values. No bound on the sum of `pair_mask` on one device may be relied on, other than what follows from the above.
Results may differ from the reference program's by a relative error of at most 0.001.
The reference program's roundings to bfloat16 on the way (of `normed`, `hidden`, `half`, `grad_logits`, `grad_flip` and `grad_pair`) count: a program that leaves them out, or rounds other values in their place, can miss the bound.
Values may be sent and summed in bfloat16 or wider, within the bound.
No kernel may reach another device: no remote copies, remote signals or barrier semaphores. Data moves between devices by JAX's collectives and lax.ppermute only.
A program may use at most 64 MiB of HBM per device.

```python
import math
import jax
import jax.numpy as jnp
from jax import lax

C_Z = 128
C_HID = 512
BINS = 64
N_TOK = 1024


def plant(array, key, smallest, largest):
    place = [jax.random.randint(jax.random.fold_in(key, axis), (), 0, length) for axis, length in enumerate(array.shape)]
    widest = array.shape.index(max(array.shape))
    neighbour = place[:widest] + [(place[widest] + 1) % array.shape[widest]] + place[widest + 1:]
    return array.at[tuple(place)].set(smallest).at[tuple(neighbour)].set(largest)


def steps_of(own_key, dims, split, smallest, high):
    loudness = 1.0
    for position, parts in split:
        steps = jax.random.uniform(jax.random.fold_in(jax.random.fold_in(own_key, 6), position), (parts,), jnp.float32, smallest / len(split), high / len(split))
        loudness = loudness * jnp.repeat(jnp.exp(steps), dims[position] // parts).reshape((-1,) + (1,) * (len(dims) - 1 - position))
    return loudness


def bell_draw(key, extent, scale, reach, cuts=(), kind=jnp.bfloat16):
    factor_of = steps_of(key, extent, cuts, -0.22, 0.18) if cuts else 1.0
    result = jax.random.normal(key, extent, jnp.float32) * scale * factor_of
    return jnp.minimum(jnp.maximum(result, -reach), reach).astype(kind)


def setup_inputs(seed: int = 0) -> dict:
    streams_of = jax.random.split(jax.random.key(seed), 10)
    return {
        "pair": bell_draw(streams_of[0], (N_TOK, N_TOK, C_Z), 1.0, 6.0, ((0, 16), (1, 8))),
        "ln_gain": jnp.clip(1.0 + 0.18 * jax.random.normal(streams_of[1], (C_Z,), jnp.float32), 0.1, 1.9),
        "ln_bias": bell_draw(streams_of[2], (C_Z,), 0.5, 3.0, (), jnp.float32),
        "gate_weight": bell_draw(streams_of[3], (C_Z, C_HID), C_Z ** -0.5, 0.5),
        "up_weight": bell_draw(streams_of[4], (C_Z, C_HID), C_Z ** -0.5, 0.5),
        "out_weight": bell_draw(streams_of[5], (C_HID, C_Z), C_HID ** -0.5, 0.25),
        "head_weight": bell_draw(streams_of[6], (C_Z, BINS), (C_Z // 4) ** -0.5, 1.0),
        "targets": plant(jax.random.randint(streams_of[7], (N_TOK, N_TOK), 0, BINS), jax.random.fold_in(streams_of[7], 1), 0, BINS - 1).astype(jnp.int32),
        "pair_mask": plant((jax.random.randint(streams_of[8], (N_TOK, N_TOK), 0, 4) < 3).astype(jnp.int32), jax.random.fold_in(streams_of[8], 1), 0, 1),
    }


EPSILON = 1e-05

def normalize(rows_in, ln_gain, ln_bias):
    values = rows_in.astype(jnp.float32)
    centered = values - lax.optimization_barrier(jnp.mean(values, axis=-1, keepdims=True))
    variance = lax.optimization_barrier(jnp.mean(centered * centered, axis=-1, keepdims=True))
    unit_rows = centered * lax.rsqrt(variance + EPSILON)
    normed = (unit_rows * ln_gain + ln_bias).astype(jnp.bfloat16)
    return (unit_rows, normed)

def inner(left, right):
    return lax.dot_general(left, right, (((0,), (0,)), ((), ())), preferred_element_type=jnp.float32)

def advance(rows_in, ln_gain, ln_bias, gate_weight, up_weight, out_weight):
    unit_rows, normed = normalize(rows_in, ln_gain, ln_bias)
    gate_pre = jnp.dot(normed, gate_weight, preferred_element_type=jnp.float32)
    up_pre = jnp.dot(normed, up_weight, preferred_element_type=jnp.float32)
    hidden = (jax.nn.silu(gate_pre) * up_pre).astype(jnp.bfloat16)
    update = jnp.dot(hidden, out_weight, preferred_element_type=jnp.float32)
    return (rows_in.astype(jnp.float32) + update).astype(jnp.bfloat16)

def retreat(totals, rows_in, grad_rows, ln_gain, ln_bias, gate_weight, up_weight, out_weight):
    unit_rows, normed = normalize(rows_in, ln_gain, ln_bias)
    gate_pre = jnp.dot(normed, gate_weight, preferred_element_type=jnp.float32)
    up_pre = jnp.dot(normed, up_weight, preferred_element_type=jnp.float32)
    squashed = jax.nn.sigmoid(gate_pre)
    silu_val = gate_pre * squashed
    hidden = (silu_val * up_pre).astype(jnp.bfloat16)
    grad_hidden = jnp.dot(grad_rows, out_weight.T, preferred_element_type=jnp.float32)
    grad_gate_pre = (grad_hidden * up_pre * squashed * (1.0 + gate_pre * (1.0 - squashed))).astype(jnp.bfloat16)
    grad_up_pre = (grad_hidden * silu_val).astype(jnp.bfloat16)
    grad_normed = jnp.dot(grad_gate_pre, gate_weight.T, preferred_element_type=jnp.float32) + jnp.dot(grad_up_pre, up_weight.T, preferred_element_type=jnp.float32)
    sum_gain, sum_bias, sum_gate, sum_up, sum_out = totals
    return (sum_gain + lax.optimization_barrier(jnp.sum(grad_normed * unit_rows, axis=0)), sum_bias + lax.optimization_barrier(jnp.sum(grad_normed, axis=0)), sum_gate + inner(normed, grad_gate_pre), sum_up + inner(normed, grad_up_pre), sum_out + inner(hidden, grad_rows))

def reference(pair, ln_gain, ln_bias, gate_weight, up_weight, out_weight, head_weight, targets, pair_mask):
    tokens = N_TOK
    width = pair.shape[-1]
    block_rows = math.gcd(tokens, 16)
    count = tokens // block_rows
    blocks = pair.reshape(count, block_rows * tokens, width)

    def forward_one(rows_in):
        return advance(rows_in, ln_gain, ln_bias, gate_weight, up_weight, out_weight)
    pair_out = lax.map(forward_one, blocks).reshape(pair.shape)
    half = jnp.dot(pair_out, head_weight, preferred_element_type=jnp.float32).astype(jnp.bfloat16)
    logits = half.astype(jnp.float32) + jnp.swapaxes(half, 0, 1).astype(jnp.float32)
    bins = logits.shape[-1]
    one_hot = (targets[..., None] == jnp.arange(bins, dtype=jnp.int32)).astype(jnp.float32)
    log_total = jnp.log(lax.optimization_barrier(jnp.sum(jnp.exp(logits), axis=-1)))
    weights_mask = pair_mask.astype(jnp.float32)
    nll = log_total - lax.optimization_barrier(jnp.sum(logits * one_hot, axis=-1))
    loss = jnp.sum(weights_mask * nll) / (tokens * tokens)
    soft_probs = jnp.exp(logits - log_total[..., None])
    grad_logits = (weights_mask[..., None] * (soft_probs - one_hot) / tokens).astype(jnp.bfloat16)
    grad_flip = jnp.swapaxes(grad_logits, 0, 1)
    flat_out = pair_out.reshape(-1, width)
    grad_head = inner(flat_out, grad_logits.reshape(-1, bins)) + inner(flat_out, grad_flip.reshape(-1, bins))
    head_back = head_weight.T
    grad_pair = (jnp.dot(grad_logits, head_back, preferred_element_type=jnp.float32) + jnp.dot(grad_flip, head_back, preferred_element_type=jnp.float32)).astype(jnp.bfloat16)
    grad_blocks = grad_pair.reshape(count, block_rows * tokens, width)
    hidden_width = gate_weight.shape[1]
    start = (jnp.zeros((width,), jnp.float32), jnp.zeros((width,), jnp.float32), jnp.zeros((width, hidden_width), jnp.float32), jnp.zeros((width, hidden_width), jnp.float32), jnp.zeros((hidden_width, width), jnp.float32))

    def backward_one(totals, inputs):
        return (retreat(totals, inputs[0], inputs[1], ln_gain, ln_bias, gate_weight, up_weight, out_weight), None)
    totals, unused = lax.scan(backward_one, start, (blocks, grad_blocks))
    return (pair_out, loss, totals[0], totals[1], totals[2], totals[3], totals[4], grad_head)
```

```python
import functools

import jax
import jax.numpy as jnp
from jax import lax
from jax.experimental import pallas as pl
from jax.experimental.pallas import tpu as pltpu
from jax.sharding import PartitionSpec as P

EPSILON = 1e-05
F32 = jnp.float32
BF16 = jnp.bfloat16
AXES = ("row", "col")

SIDE = 64
GROUP = 8
F_COLS = 16
B_GROUPS = 2


def dot(left, right, dims=((1,), (0,))):
    return lax.dot_general(left, right, (dims, ((), ())), preferred_element_type=F32)


def normalize(rows_in, gain, bias):
    values = rows_in.astype(F32)
    centered = values - jnp.mean(values, axis=-1, keepdims=True)
    variance = jnp.mean(centered * centered, axis=-1, keepdims=True)
    unit_rows = centered * lax.rsqrt(variance + EPSILON)
    return unit_rows, (unit_rows * gain + bias).astype(BF16)


def sigmoid(values):
    return 0.5 * jnp.tanh(0.5 * values) + 0.5


def forward_body(which, pair, gain, bias, w_in, w_out, head_two, *rest):
    pair_out, send, wide = rest[-3:]
    hid = w_out.shape[0]
    rows_in = pair[...].reshape(SIDE * F_COLS, 128)
    count = 4
    size = SIDE * F_COLS // count
    for k in range(count):
        part = rows_in[k * size : (k + 1) * size]
        _, normed = normalize(part, gain[...], bias[...])
        gate_pre = dot(normed, w_in[:, :hid])
        up_pre = dot(normed, w_in[:, hid:])
        hidden = (gate_pre * sigmoid(gate_pre) * up_pre).astype(BF16)
        result = (part.astype(F32) + dot(hidden, w_out[...])).astype(BF16)
        pair_out[k * size // F_COLS : (k + 1) * size // F_COLS] = result.reshape(
            size // F_COLS, 1, F_COLS, 128
        )
        wide[k * size : (k + 1) * size, :] = result.astype(F32)
    for grp in range(F_COLS // GROUP):
        left, right = [
            jnp.concatenate(
                [
                    wide[pl.ds(grp * GROUP + shift + a, SIDE, stride=F_COLS), :]
                    for a in range(GROUP // 2)
                ],
                axis=0,
            )
            for shift in (0, GROUP // 2)
        ]
        both = jnp.concatenate([left, right], axis=1).astype(BF16)
        rows = SIDE * GROUP // 2
        send[grp * rows : (grp + 1) * rows, :] = dot(both, head_two[...]).astype(BF16)


def forward_call(which, pair4, gain, bias, w_in, w_out, head_two, partial=None):
    block = pl.BlockSpec((SIDE, 1, F_COLS, 128), lambda g, w: (0, w[0], g, 0))
    whole = lambda a: pl.BlockSpec(a.shape, lambda g, w: (0,) * a.ndim)
    in_specs = [block] + [whole(a) for a in (gain, bias, w_in, w_out, head_two)]
    args = [pair4, gain, bias, w_in, w_out, head_two]
    alias = {}
    if partial is not None:
        in_specs.append(pl.BlockSpec(memory_space=pl.ANY))
        args.append(partial)
        alias = {7: 0}
    steps = SIDE // F_COLS
    rows = SIDE * F_COLS // 2
    return pl.pallas_call(
        forward_body,
        out_shape=(
            jax.ShapeDtypeStruct(pair4.shape, BF16),
            jax.ShapeDtypeStruct((rows * steps, 128), BF16),
        ),
        grid_spec=pltpu.PrefetchScalarGridSpec(
            num_scalar_prefetch=1,
            grid=(steps,),
            in_specs=in_specs,
            out_specs=(block, pl.BlockSpec((rows, 128), lambda g, w: (g, 0))),
            scratch_shapes=[pltpu.VMEM((SIDE * F_COLS, 128), F32)],
        ),
        input_output_aliases=alias,
        compiler_params=pltpu.CompilerParams(dimension_semantics=("arbitrary",)),
        name="forward",
    )(which, *args)


def code_of(word):
    return (jnp.bitwise_and(word, 65535) + 64 * jnp.right_shift(word, 16)).astype(F32).astype(BF16)


def backward_body(
    which, pair, pair_out, mirror, own_code, mirror_code, gain, bias, w_in, w_out, head_two, *rest
):
    if len(rest) > 8:
        earlier, rest = rest[:4], rest[4:]
    else:
        earlier = None
    g_in, g_out, g_head, g_small, s_normed, s_grad_in, s_hidden, s_pair = rest
    hid = w_out.shape[0]
    step = pl.program_id(0)
    rows = SIDE * GROUP // 2

    @pl.when(step == 0)
    def _():
        if earlier is None:
            for ref in (g_in, g_out, g_head, g_small):
                ref[...] = jnp.zeros_like(ref)
        else:
            for ref, old in zip((g_in, g_out, g_head, g_small), earlier):
                ref[...] = old[...]

    lane = lax.broadcasted_iota(jnp.int32, (rows, 128), 1)
    wanted = (jnp.bitwise_and(lane, 63) + 64).astype(F32)
    lane_row = lax.broadcasted_iota(jnp.int32, (128, 128), 0)
    lane_col = lax.broadcasted_iota(jnp.int32, (128, 128), 1)
    same = (lane_row // 64 == lane_col // 64).astype(F32).astype(BF16)
    sum_bins = jnp.concatenate([same, same], axis=0)
    own = code_of(own_code[...])
    other = code_of(mirror_code[...])
    pick_n = lax.broadcasted_iota(jnp.int32, (SIDE, 512), 1)
    pick_k = lax.broadcasted_iota(jnp.int32, (SIDE, 512), 0)
    pick_base = pick_n // 128 + (GROUP // 2) * (jnp.bitwise_and(pick_n, 127) // 64)

    for grp in range(B_GROUPS):
        at = grp * 2 * rows
        x_out = pair_out[grp * GROUP : (grp + 1) * GROUP].reshape(2 * rows, 128)
        both = jnp.concatenate([x_out[:rows], x_out[rows:]], axis=1)
        half = dot(both, head_two[...]).astype(BF16)
        logits = half.astype(F32) + mirror[grp * rows : (grp + 1) * rows, :].astype(F32)
        expo = 0.5 * jnp.exp(logits)
        high = expo.astype(BF16)
        low = (expo - high.astype(F32)).astype(BF16)
        total = dot(jnp.concatenate([high, low], axis=1), sum_bins)
        log_total = jnp.log(total) + 0.6931471805599453
        soft = jnp.exp(logits - log_total)
        pick = (pick_k == pick_base + GROUP * (step * B_GROUPS + grp)).astype(F32).astype(BF16)
        codes = []
        for spread in (dot(own, pick, ((0,), (0,))), dot(other, pick)):
            codes.append(
                jnp.concatenate([spread[:, 128 * a : 128 * (a + 1)] for a in range(4)], axis=0)
            )
        scale = 1.0 / 1024.0
        hit = codes[0] == wanted
        grads = [
            (scale * (jnp.where(c >= 63.5, soft, 0.0) - jnp.where(c == wanted, 1.0, 0.0))).astype(
                BF16
            )
            for c in codes
        ]
        loss_part = jnp.where(hit, log_total - logits, 0.0)
        grad_both = jnp.concatenate(grads, axis=1)
        g_head[...] += dot(both, grad_both, ((0,), (0,)))
        head_rows = jnp.concatenate([head_two[...], head_two[...]], axis=1)
        grad_pair = dot(grad_both, head_rows, ((1,), (1,))).astype(BF16)
        grad_pair = jnp.concatenate([grad_pair[:, :128], grad_pair[:, 128:]], axis=0)
        s_pair[at : at + 2 * rows, :] = grad_pair

        x_in = pair[grp * GROUP : (grp + 1) * GROUP].reshape(2 * rows, 128)
        unit_rows, normed = normalize(x_in, gain[...], bias[...])
        s_normed[at : at + 2 * rows, :] = normed
        gate_pre = dot(normed, w_in[:, :hid])
        up_pre = dot(normed, w_in[:, hid:])
        grad_hidden = dot(grad_pair, w_out[...], ((1,), (1,)))
        squashed = sigmoid(gate_pre)
        silu_val = gate_pre * squashed
        s_hidden[at : at + 2 * rows, :] = (silu_val * up_pre).astype(BF16)
        slope = squashed * (1.0 + gate_pre * (1.0 - squashed))
        s_grad_in[at : at + 2 * rows, :hid] = (grad_hidden * up_pre * slope).astype(BF16)
        s_grad_in[at : at + 2 * rows, hid:] = (grad_hidden * silu_val).astype(BF16)
        grad_normed = dot(s_grad_in[at : at + 2 * rows, :], w_in[...], ((1,), (1,)))
        fold = lambda v: jnp.sum(v.reshape(-1, 8, 128), axis=0)
        g_small[0:8, :] += fold(grad_normed * unit_rows)
        g_small[8:16, :] += fold(grad_normed)
        g_small[16:24, :] += fold(loss_part)
    g_in[...] += dot(s_normed[...], s_grad_in[...], ((0,), (0,)))
    g_out[...] += dot(s_pair[...], s_hidden[...], ((0,), (0,)))


def backward_call(
    which, pair4, pair_out4, mirror, own_code, mirror_code, gain, bias, w_in, w_out, head_two,
    earlier=None,
):
    wide, hid = w_in.shape[1], w_out.shape[0]
    block = pl.BlockSpec((GROUP * B_GROUPS, 1, SIDE, 128), lambda g, w: (g, w[0], 0, 0))
    whole = lambda a: pl.BlockSpec(a.shape, lambda g, w: (0,) * len(a.shape))
    rows = SIDE * GROUP // 2 * B_GROUPS
    fixed = (own_code, mirror_code, gain, bias, w_in, w_out, head_two)
    in_specs = [block, block, pl.BlockSpec((rows, 128), lambda g, w: (g, 0))]
    in_specs += [whole(a) for a in fixed]
    args = [pair4, pair_out4, mirror, *fixed]
    outs = (
        jax.ShapeDtypeStruct((128, wide), F32),
        jax.ShapeDtypeStruct((128, hid), F32),
        jax.ShapeDtypeStruct((256, 256), F32),
        jax.ShapeDtypeStruct((24, 128), F32),
    )
    if earlier is not None:
        in_specs += [whole(a) for a in outs]
        args += list(earlier)
    return pl.pallas_call(
        backward_body,
        out_shape=outs,
        grid_spec=pltpu.PrefetchScalarGridSpec(
            num_scalar_prefetch=1,
            grid=(SIDE // (GROUP * B_GROUPS),),
            in_specs=in_specs,
            out_specs=tuple(whole(a) for a in outs),
            scratch_shapes=[
                pltpu.VMEM((2 * rows, 128), BF16),
                pltpu.VMEM((2 * rows, wide), BF16),
                pltpu.VMEM((2 * rows, hid), BF16),
                pltpu.VMEM((2 * rows, 128), BF16),
            ],
        ),
        compiler_params=pltpu.CompilerParams(dimension_semantics=("arbitrary",)),
        name="backward",
    )(which, *args)


def shards(
    pair, ln_gain, ln_bias, gate_weight, up_weight, out_weight, head_weight, targets, pair_mask
):
    rows_tile, cols_tile, width = pair.shape
    row_count, col_count = lax.axis_size("row"), lax.axis_size("col")
    tokens = rows_tile * row_count
    hid = gate_weight.shape[1]
    bins = head_weight.shape[1]
    row = lax.axis_index("row")
    parity = lax.rem(row, 2)
    swap = [[], []]
    for r in range(row_count):
        for c in range(col_count):
            for turn in range(2):
                h = (r + turn) % 2
                swap[turn].append((r * col_count + c, (2 * c + h) * col_count + r // 2))

    words = targets + 65536 * pair_mask
    tile_words = lax.all_to_all(words, "col", split_axis=1, concat_axis=0, tiled=True)
    tile_words = tile_words.reshape(rows_tile, 2, SIDE)

    gain, bias = ln_gain.reshape(1, width), ln_bias.reshape(1, width)
    w_in = jnp.concatenate([gate_weight, up_weight], axis=1)
    blank = jnp.zeros_like(head_weight)
    head_two = jnp.concatenate(
        [
            jnp.concatenate([head_weight, blank], axis=1),
            jnp.concatenate([blank, head_weight], axis=1),
        ],
        axis=0,
    )
    pair4 = pair.reshape(rows_tile, 2, SIDE, width)
    which = [(parity + turn) % 2 for turn in range(2)]
    which = [w.astype(jnp.int32).reshape(1) for w in which]
    weights = (gain, bias, w_in, out_weight, head_two)

    out4, sent0 = forward_call(which[0], pair4, *weights)
    mirror0 = lax.ppermute(sent0, AXES, swap[0])
    own = [
        lax.dynamic_index_in_dim(tile_words, which[turn][0], 1, keepdims=False)
        for turn in range(2)
    ]
    theirs = [lax.ppermute(own[turn], AXES, swap[turn]) for turn in range(2)]
    out4, sent1 = forward_call(which[1], pair4, *weights, partial=out4)
    mirror1 = lax.ppermute(sent1, AXES, swap[1])
    part = backward_call(which[0], pair4, out4, mirror0, own[0], theirs[0], *weights)
    part = backward_call(which[1], pair4, out4, mirror1, own[1], theirs[1], *weights, earlier=part)
    g_in, g_out, g_head, g_small = part
    head_sum = (
        g_head[:128, :bins]
        + g_head[:128, 128 : 128 + bins]
        + g_head[128:, bins:128]
        + g_head[128:, 128 + bins :]
    )
    flat = jnp.concatenate(
        [
            g_in.reshape(-1),
            g_out.reshape(-1),
            head_sum.reshape(-1),
            g_small.reshape(-1),
        ]
    )
    devices = row_count * col_count
    unit = devices * 1024
    length = flat.shape[0]
    padded = -(-length // unit) * unit
    flat = jnp.pad(flat, (0, padded - length)).reshape(devices, -1, 128)
    pieces = lax.all_to_all(flat, AXES, split_axis=0, concat_axis=0, tiled=True)
    mine = jnp.sum(pieces, axis=0, keepdims=True)
    mine = jnp.broadcast_to(mine, pieces.shape)
    summed = lax.all_to_all(mine, AXES, split_axis=0, concat_axis=0, tiled=True).reshape(-1)
    cut = [0]
    for size in (g_in.size, g_out.size, head_sum.size, g_small.size):
        cut.append(cut[-1] + size)
    s_in = summed[cut[0] : cut[1]].reshape(g_in.shape)
    s_out = summed[cut[1] : cut[2]].reshape(g_out.shape).T
    s_head = summed[cut[2] : cut[3]].reshape(head_sum.shape)
    small = jnp.sum(summed[cut[3] : cut[4]].reshape(3, 8, 128), axis=1)
    loss = jnp.sum(small[2]) / (tokens * tokens)
    pair_out = out4.reshape(pair.shape)
    return (pair_out, loss, small[0], small[1], s_in[:, :hid], s_in[:, hid:], s_out, s_head)


def solution(mesh):
    placed = (
        P("row", "col", None),
        P(),
        P(),
        P(),
        P(),
        P(),
        P(),
        P(AXES, None),
        P(AXES, None),
    )
    return jax.shard_map(
        shards,
        mesh=mesh,
        in_specs=placed,
        out_specs=(P("row", "col", None), P(), P(), P(), P(), P(), P(), P()),
        check_vma=False,
    )
```

```python
import jax
import jax.numpy as jnp
from jax import lax
from jax.experimental import pallas as pl
from jax.experimental.pallas import tpu as pltpu
from jax.sharding import PartitionSpec as P

EPSILON = 1e-05
F32 = jnp.float32
BF16 = jnp.bfloat16
AXES = ("row", "col")

SIDE = 64
PARTS = 2
GROUP = 8
F_COLS = 16
B_GROUPS = 2
ROWS = SIDE * GROUP // 2

ROUTES = ((0, 0, 1), (0, 0, 3), (0, 2, 0), None)


def chip_of(device):
    r, c = divmod(device, 8)
    return (c // 2, (r % 8) // 2, (c % 2) * 2 + r // 8), r % 2


def device_at(chip, core):
    x, y, z = chip
    return ((z % 2) * 8 + y * 2 + core) * 8 + x * 2 + z // 2


def mirror_of(device, turn):
    r, c = divmod(device, 8)
    return (2 * c + (r + turn) % 2) * 8 + r // 2


def shifted(device, shift):
    chip, core = chip_of(device)
    return device_at(tuple((a + b) % 4 for a, b in zip(chip, shift)), core)


def send_to_mirror(value, turn, route):
    devices = range(128)
    if route is None:
        return lax.ppermute(value, AXES, [(d, mirror_of(d, turn)) for d in devices])
    value = lax.ppermute(value, AXES, [(d, shifted(d, route)) for d in devices])
    return lax.ppermute(value, AXES, [(shifted(d, route), mirror_of(d, turn)) for d in devices])


def dot(left, right, dims=((1,), (0,))):
    return lax.dot_general(left, right, (dims, ((), ())), preferred_element_type=F32)


NT = ((1,), (1,))
TN = ((0,), (0,))


def normalize(rows_in, gain, bias):
    values = rows_in.astype(F32)
    centered = values - jnp.mean(values, axis=-1, keepdims=True)
    variance = jnp.mean(centered * centered, axis=-1, keepdims=True)
    unit_rows = centered * lax.rsqrt(variance + EPSILON)
    return unit_rows, (unit_rows * gain + bias).astype(BF16)


def sigmoid(values):
    return 0.5 * jnp.tanh(0.5 * values) + 0.5


def head_square(head_t):
    blank = jnp.zeros_like(head_t)
    return jnp.concatenate(
        [
            jnp.concatenate([head_t, blank], axis=1),
            jnp.concatenate([blank, head_t], axis=1),
        ],
        axis=0,
    )


def forward_body(which, pair, gain, bias, w_gate, w_up, w_out, head_t, *rest):
    pair_out, send, wide = rest[-3:]
    rows_in = pair[...].reshape(SIDE * F_COLS, 128)
    count = 4
    size = SIDE * F_COLS // count
    for k in range(count):
        part = rows_in[k * size : (k + 1) * size]
        _, normed = normalize(part, gain[...], bias[...])
        gate_pre = dot(normed, w_gate[...])
        up_pre = dot(normed, w_up[...])
        hidden = (gate_pre * sigmoid(gate_pre) * up_pre).astype(BF16)
        result = (part.astype(F32) + dot(hidden, w_out[...])).astype(BF16)
        pair_out[k * size // F_COLS : (k + 1) * size // F_COLS] = result.reshape(
            size // F_COLS, 1, F_COLS, 128
        )
        wide[k * size : (k + 1) * size, :] = result.astype(F32)
    head_two = head_square(head_t[...])
    for grp in range(F_COLS // GROUP):
        left, right = [
            jnp.concatenate(
                [
                    wide[pl.ds(grp * GROUP + shift + a, SIDE, stride=F_COLS), :]
                    for a in range(GROUP // 2)
                ],
                axis=0,
            )
            for shift in (0, GROUP // 2)
        ]
        both = jnp.concatenate([left, right], axis=1).astype(BF16)
        send[grp * ROWS : (grp + 1) * ROWS, :] = dot(both, head_two, NT).astype(BF16)


def whole(a):
    return pl.BlockSpec(a.shape, lambda g, w: (0,) * len(a.shape))


def forward_call(which, part, pair4, weights, partial=None, after=None):
    steps = SIDE // PARTS // F_COLS
    block = pl.BlockSpec((SIDE, 1, F_COLS, 128), lambda g, w: (0, w[0], part * steps + g, 0))
    in_specs = [block] + [whole(a) for a in weights]
    args = [pair4, *weights]
    alias = {}
    if partial is not None:
        in_specs.append(pl.BlockSpec(memory_space=pl.ANY))
        alias = {1 + len(args): 0}
        args.append(partial)
    if after is not None:
        in_specs.append(pl.BlockSpec(memory_space=pl.ANY))
        args.append(after)
    rows = ROWS * F_COLS // GROUP
    pairs = SIDE * SIDE // PARTS
    return pl.pallas_call(
        forward_body,
        out_shape=(
            jax.ShapeDtypeStruct(pair4.shape, BF16),
            jax.ShapeDtypeStruct((rows * steps, 128), BF16),
        ),
        grid_spec=pltpu.PrefetchScalarGridSpec(
            num_scalar_prefetch=1,
            grid=(steps,),
            in_specs=in_specs,
            out_specs=(block, pl.BlockSpec((rows, 128), lambda g, w: (g, 0))),
            scratch_shapes=[pltpu.VMEM((SIDE * F_COLS, 128), F32)],
        ),
        input_output_aliases=alias,
        cost_estimate=pl.CostEstimate(
            flops=pairs * 2 * 128 * 512 * 3, transcendentals=pairs * 512, bytes_accessed=pairs * 640
        ),
        compiler_params=pltpu.CompilerParams(dimension_semantics=("arbitrary",)),
        name="forward",
    )(which, *args)


def code_of(word):
    return (jnp.bitwise_and(word, 65535) + 64 * jnp.right_shift(word, 16)).astype(F32).astype(BF16)


def backward_body(first_group, first, last, which, *refs):
    pair, pair_out, mirror, own_code, mirror_code = refs[:5]
    gain, bias, w_gate, w_up, w_out, head_t = refs[5:11]
    rest = list(refs[11:])
    earlier = None
    if not first:
        earlier, rest = rest[:4], rest[4:]
    if last:
        keep, send = rest[:2]
        rest = rest[2:]
    g_in, g_out, g_head, g_small, s_normed, s_grad_in, s_hidden, s_pair = rest
    sums = (g_in, g_out, g_head, g_small)
    hid = w_out.shape[0]
    step = pl.program_id(0)

    @pl.when(step == 0)
    def _():
        for k, ref in enumerate(sums):
            ref[...] = jnp.zeros_like(ref) if first else earlier[k][...]

    lane = lax.broadcasted_iota(jnp.int32, (ROWS, 128), 1)
    wanted = (jnp.bitwise_and(lane, 63) + 64).astype(F32)
    lane_row = lax.broadcasted_iota(jnp.int32, (128, 128), 0)
    lane_col = lax.broadcasted_iota(jnp.int32, (128, 128), 1)
    same = (lane_row // 64 == lane_col // 64).astype(F32).astype(BF16)
    sum_bins = jnp.concatenate([same, same], axis=0)
    head_two = head_square(head_t[...])
    head_four = jnp.concatenate([head_two, head_two], axis=0)
    own = code_of(own_code[...])
    other = code_of(mirror_code[...])
    pick_n = lax.broadcasted_iota(jnp.int32, (SIDE, 512), 1)
    pick_k = lax.broadcasted_iota(jnp.int32, (SIDE, 512), 0)
    pick_base = pick_n // 128 + (GROUP // 2) * (jnp.bitwise_and(pick_n, 127) // 64)

    for grp in range(B_GROUPS):
        at = slice(grp * 2 * ROWS, (grp + 1) * 2 * ROWS)
        x_out = pair_out[grp * GROUP : (grp + 1) * GROUP].reshape(2 * ROWS, 128)
        both = jnp.concatenate([x_out[:ROWS], x_out[ROWS:]], axis=1)
        half = dot(both, head_two, NT).astype(BF16)
        logits = half.astype(F32) + mirror[grp * ROWS : (grp + 1) * ROWS, :].astype(F32)
        expo = 0.5 * jnp.exp(logits)
        high = expo.astype(BF16)
        low = (expo - high.astype(F32)).astype(BF16)
        total = dot(jnp.concatenate([high, low], axis=1), sum_bins)
        log_total = jnp.log(total) + 0.6931471805599453
        soft = jnp.exp(logits - log_total)
        group = first_group + step * B_GROUPS + grp
        pick = (pick_k == pick_base + GROUP * group).astype(F32).astype(BF16)
        codes = []
        for spread in (dot(own, pick, TN), dot(other, pick)):
            codes.append(
                jnp.concatenate([spread[:, 128 * a : 128 * (a + 1)] for a in range(4)], axis=0)
            )
        grads = [
            (
                (jnp.where(c >= 63.5, soft, 0.0) - jnp.where(c == wanted, 1.0, 0.0)) * (1.0 / 1024)
            ).astype(BF16)
            for c in codes
        ]
        loss_part = jnp.where(codes[0] == wanted, log_total - logits, 0.0)
        grad_both = jnp.concatenate(grads, axis=1)
        g_head[...] += dot(grad_both, both, TN)
        grad_pair = dot(grad_both, head_four).astype(BF16)
        grad_pair = jnp.concatenate([grad_pair[:, :128], grad_pair[:, 128:]], axis=0)
        s_pair[at, :] = grad_pair

        x_in = pair[grp * GROUP : (grp + 1) * GROUP].reshape(2 * ROWS, 128)
        unit_rows, normed = normalize(x_in, gain[...], bias[...])
        s_normed[at, :] = normed
        gate_pre = dot(normed, w_gate[...])
        up_pre = dot(normed, w_up[...])
        grad_hidden = dot(grad_pair, w_out[...], NT)
        squashed = sigmoid(gate_pre)
        silu_val = gate_pre * squashed
        s_hidden[at, :] = (silu_val * up_pre).astype(BF16)
        slope = squashed * (1.0 + gate_pre * (1.0 - squashed))
        s_grad_in[at, :hid] = (grad_hidden * up_pre * slope).astype(BF16)
        s_grad_in[at, hid:] = (grad_hidden * silu_val).astype(BF16)
        grad_normed = dot(s_grad_in[at, :hid], w_gate[...], NT)
        grad_normed += dot(s_grad_in[at, hid:], w_up[...], NT)
        fold = lambda v: jnp.sum(v.reshape(-1, 8, 128), axis=0)
        g_small[0:8, :] += fold(grad_normed * unit_rows)
        g_small[8:16, :] += fold(grad_normed)
        g_small[16:24, :] += fold(loss_part)
    g_in[...] += dot(s_normed[...], s_grad_in[...], TN)
    g_out[...] += dot(s_pair[...], s_hidden[...], TN)

    if not last:
        return

    def put_in(ref):
        for k in range(8):
            ref[128 * k : 128 * (k + 1), :] = g_in[:, 128 * k : 128 * (k + 1)]

    def put_rest(ref):
        for k in range(4):
            ref[128 * k : 128 * (k + 1), :] = g_out[:, 128 * k : 128 * (k + 1)].T
        ref[512:576, :] = (
            g_head[0:64, 0:128]
            + g_head[64:128, 128:256]
            + g_head[128:192, 0:128]
            + g_head[192:256, 128:256]
        )
        small = [jnp.sum(g_small[8 * k : 8 * k + 8, :], axis=0, keepdims=True) for k in range(3)]
        ref[576:584, :] = jnp.concatenate(small + [jnp.zeros((5, 128), F32)], axis=0)
        ref[584:1024, :] = jnp.zeros((440, 128), F32)

    at_end = step == pl.num_programs(0) - 1

    @pl.when(jnp.logical_and(at_end, which[1] == 0))
    def _():
        put_in(keep)
        put_rest(send)

    @pl.when(jnp.logical_and(at_end, which[1] != 0))
    def _():
        put_in(send)
        put_rest(keep)


def backward_call(
    which, part, pair4, pair_out4, mirror, own_code, mirror_code, weights, earlier, last
):
    wide, hid = 2 * weights[2].shape[1], weights[4].shape[0]
    steps = SIDE // PARTS // (GROUP * B_GROUPS)
    block = pl.BlockSpec(
        (GROUP * B_GROUPS, 1, SIDE, 128), lambda g, w: (part * steps + g, w[0], 0, 0)
    )
    rows = ROWS * B_GROUPS
    fixed = (own_code, mirror_code, *weights)
    in_specs = [block, block, pl.BlockSpec((rows, 128), lambda g, w: (g, 0))]
    in_specs += [whole(a) for a in fixed]
    args = [pair4, pair_out4, mirror, *fixed]
    sums = [(128, wide), (128, hid), (256, 256), (24, 128)]
    if earlier is not None:
        in_specs += [whole(a) for a in earlier]
        args += list(earlier)
    outs = [jax.ShapeDtypeStruct(s, F32) for s in ([(1024, 128)] * 2 if last else sums)]
    scratch = [pltpu.VMEM(s, F32) for s in sums] if last else []
    scratch += [
        pltpu.VMEM((2 * rows, 128), BF16),
        pltpu.VMEM((2 * rows, wide), BF16),
        pltpu.VMEM((2 * rows, hid), BF16),
        pltpu.VMEM((2 * rows, 128), BF16),
    ]
    pairs = SIDE * SIDE // PARTS

    def body(*refs):
        backward_body(part * steps * B_GROUPS, earlier is None, last, *refs)

    return pl.pallas_call(
        body,
        out_shape=tuple(outs),
        grid_spec=pltpu.PrefetchScalarGridSpec(
            num_scalar_prefetch=1,
            grid=(steps,),
            in_specs=in_specs,
            out_specs=tuple(whole(a) for a in outs),
            scratch_shapes=scratch,
        ),
        cost_estimate=pl.CostEstimate(
            flops=pairs * 2 * 128 * 512 * 8, transcendentals=pairs * 640, bytes_accessed=pairs * 640
        ),
        compiler_params=pltpu.CompilerParams(dimension_semantics=("arbitrary",)),
        name="backward",
    )(which, *args)


def unpack_body(core, mine, other, d_gate, d_up, d_out, d_head, d_gain, d_bias, loss):
    def fill(lower, upper):
        for k in range(4):
            d_gate[:, 128 * k : 128 * (k + 1)] = lower[128 * k : 128 * (k + 1), :]
            d_up[:, 128 * k : 128 * (k + 1)] = lower[512 + 128 * k : 640 + 128 * k, :]
        d_out[...] = upper[0:512, :]
        d_head[...] = upper[512:576, :]
        d_gain[...] = upper[576:577, :]
        d_bias[...] = upper[577:578, :]
        loss[0, 0] = jnp.sum(upper[578:579, :]) * (1.0 / 1048576)

    @pl.when(core[0] == 0)
    def _():
        fill(mine, other)

    @pl.when(core[0] != 0)
    def _():
        fill(other, mine)


def unpack_call(core, mine, other):
    shapes = [(128, 512), (128, 512), (512, 128), (64, 128), (1, 128), (1, 128), (1, 1)]
    outs = tuple(jax.ShapeDtypeStruct(s, F32) for s in shapes)
    specs = [whole(a) for a in outs[:-1]] + [pl.BlockSpec(memory_space=pltpu.SMEM)]
    return pl.pallas_call(
        unpack_body,
        out_shape=outs,
        grid_spec=pltpu.PrefetchScalarGridSpec(
            num_scalar_prefetch=1,
            grid=(1,),
            in_specs=[whole(mine), whole(other)],
            out_specs=tuple(specs),
        ),
        name="unpack",
    )(core, mine, other)


def shards(
    pair, ln_gain, ln_bias, gate_weight, up_weight, out_weight, head_weight, targets, pair_mask
):
    rows_tile, cols_tile, width = pair.shape
    row = lax.axis_index("row")
    core = lax.rem(row, 2).astype(jnp.int32)
    which = [jnp.stack([core, core]), jnp.stack([1 - core, core])]

    words = targets + 65536 * pair_mask
    with jax.named_scope("words"):
        tile_words = lax.all_to_all(words, "col", split_axis=1, concat_axis=0, tiled=True)
    blocks = tile_words.reshape(rows_tile, 2, SIDE)

    pair4 = pair.reshape(rows_tile, 2, SIDE, width)
    weights = (
        ln_gain.reshape(1, width),
        ln_bias.reshape(1, width),
        gate_weight,
        up_weight,
        out_weight,
        head_weight.T,
    )
    chunks = [(turn, part) for turn in range(2) for part in range(PARTS)]
    out4 = None
    mirrors = []
    own, theirs = [], []
    for k, (turn, part) in enumerate(chunks):
        after = tile_words if k == 1 else None
        out4, sent = forward_call(which[turn], part, pair4, weights, out4, after)
        if k == 0:
            for t in range(2):
                own.append(
                    lax.dynamic_index_in_dim(blocks, which[t][0], 1, keepdims=False)
                )
                theirs.append(send_to_mirror(own[t], t, None))
        mirrors.append(send_to_mirror(sent, turn, ROUTES[k]))
    sums = None
    for k, (turn, part) in enumerate(chunks):
        sums = backward_call(
            which[turn], part, pair4, out4, mirrors[k], own[turn], theirs[turn], weights, sums,
            k == len(chunks) - 1,
        )
    keep, send = sums
    sibling = [(d, device_at(chip_of(d)[0], 1 - chip_of(d)[1])) for d in range(128)]
    groups = [[d for d in range(128) if chip_of(d)[1] == k] for k in range(2)]
    both_cores = (keep + lax.ppermute(send, AXES, sibling)).reshape(64, 16, 128)
    pieces = lax.all_to_all(
        both_cores, AXES, split_axis=0, concat_axis=0, axis_index_groups=groups, tiled=True
    )
    mine = jnp.sum(pieces, axis=0, keepdims=True)
    mine = lax.all_to_all(
        jnp.broadcast_to(mine, pieces.shape),
        AXES,
        split_axis=0,
        concat_axis=0,
        axis_index_groups=groups,
        tiled=True,
    ).reshape(1024, 128)
    other = lax.ppermute(mine, AXES, sibling)
    d_gate, d_up, d_out, d_head, d_gain, d_bias, loss = unpack_call(core.reshape(1), mine, other)
    return (
        out4.reshape(pair.shape),
        loss.reshape(()),
        d_gain.reshape(width),
        d_bias.reshape(width),
        d_gate,
        d_up,
        d_out,
        d_head.T,
    )


def solution(mesh):
    placed = (
        P("row", "col", None),
        P(),
        P(),
        P(),
        P(),
        P(),
        P(),
        P(AXES, None),
        P(AXES, None),
    )
    return jax.shard_map(
        shards,
        mesh=mesh,
        in_specs=placed,
        out_specs=(P("row", "col", None), P(), P(), P(), P(), P(), P(), P()),
        check_vma=False,
    )
```

```python
import jax
import jax.numpy as jnp
from jax import lax
from jax.experimental import pallas as pl
from jax.experimental.pallas import tpu as pltpu
from jax.sharding import PartitionSpec as P


EPSILON = 1e-05
F32 = jnp.float32
BF16 = jnp.bfloat16
AXES = ("row", "col")

SIDE = 64
GROUP = 8
F_COLS = 16
B_GROUPS = 2
ROWS = SIDE * GROUP // 2
CHUNK_ROWS = SIDE * SIDE // 4

ROUTES = (((0, 0, 1), None), ((0, 0, 3), (0, 2, 0)))


def chip_of(device):
    r, c = divmod(device, 8)
    return (c // 2, (r % 8) // 2, (c % 2) * 2 + r // 8), r % 2


def device_at(chip, core):
    x, y, z = chip
    return ((z % 2) * 8 + y * 2 + core) * 8 + x * 2 + z // 2


def mirror_of(device, turn):
    r, c = divmod(device, 8)
    return (2 * c + (r + turn) % 2) * 8 + r // 2


def shifted(device, shift):
    chip, core = chip_of(device)
    return device_at(tuple((a + b) % 4 for a, b in zip(chip, shift)), core)


def send_to_mirror(value, turn, route):
    devices = range(128)
    if route is None:
        return lax.ppermute(value, AXES, [(d, mirror_of(d, turn)) for d in devices])
    value = lax.ppermute(value, AXES, [(d, shifted(d, route)) for d in devices])
    return lax.ppermute(value, AXES, [(shifted(d, route), mirror_of(d, turn)) for d in devices])


def dot(left, right, dims=((1,), (0,))):
    return lax.dot_general(left, right, (dims, ((), ())), preferred_element_type=F32)


NT = ((1,), (1,))
TN = ((0,), (0,))


def normalize(rows_in, gain, bias):
    values = rows_in.astype(F32)
    centered = values - jnp.mean(values, axis=-1, keepdims=True)
    variance = jnp.mean(centered * centered, axis=-1, keepdims=True)
    unit_rows = centered * lax.rsqrt(variance + EPSILON)
    return unit_rows, (unit_rows * gain + bias).astype(BF16)


def sigmoid(values):
    return 0.5 * jnp.tanh(0.5 * values) + 0.5


def head_square(head_t):
    blank = jnp.zeros_like(head_t)
    return jnp.concatenate(
        [
            jnp.concatenate([head_t, blank], axis=1),
            jnp.concatenate([blank, head_t], axis=1),
        ],
        axis=0,
    )


def block_words(words, block):
    tile = words[...]
    return jnp.where(block == 0, tile[:, :SIDE], tile[:, SIDE:])


def forward_body(turn, core, pair, gain, bias, w_gate, w_up, w_out, head_t, *rest):
    pair_out, send_a, send_b, wide = rest[-4:]
    words = rest[:-4]
    step = pl.program_id(0)
    rows_in = pair[...].reshape(SIDE * F_COLS, 128)
    count = 2
    size = SIDE * F_COLS // count
    for k in range(count):
        part = rows_in[k * size : (k + 1) * size]
        _, normed = normalize(part, gain[...], bias[...])
        gate_pre = dot(normed, w_gate[...])
        up_pre = dot(normed, w_up[...])
        hidden = (gate_pre * sigmoid(gate_pre) * up_pre).astype(BF16)
        result = (part.astype(F32) + dot(hidden, w_out[...])).astype(BF16)
        pair_out[k * size // F_COLS : (k + 1) * size // F_COLS] = result.reshape(
            size // F_COLS, 1, F_COLS, 128
        )
        wide[k * size : (k + 1) * size, :] = result.astype(F32)
    head_two = head_square(head_t[...])
    halves = []
    for grp in range(F_COLS // GROUP):
        left, right = [
            jnp.concatenate(
                [
                    wide[pl.ds(grp * GROUP + shift + a, SIDE, stride=F_COLS), :]
                    for a in range(GROUP // 2)
                ],
                axis=0,
            )
            for shift in (0, GROUP // 2)
        ]
        both = jnp.concatenate([left, right], axis=1).astype(BF16)
        halves.append(dot(both, head_two, NT).astype(BF16))
    rows = ROWS * F_COLS // GROUP
    per_chunk = CHUNK_ROWS // rows
    first_row = pl.multiple_of(lax.rem(step, per_chunk) * rows, rows)

    @pl.when(step < per_chunk)
    def _():
        send_a[pl.ds(first_row, rows), :] = jnp.concatenate(halves, axis=0)

    @pl.when(step >= per_chunk)
    def _():
        send_b[pl.ds(first_row, rows), :] = jnp.concatenate(halves, axis=0)

    if turn == 0:
        return

    @pl.when(step == 0)
    def _():
        own = block_words(words[0], lax.rem(core[0] + turn, 2))
        target = jnp.bitwise_and(own, 65535).astype(F32)
        mask = jnp.right_shift(own, 16).astype(F32)
        send_b[CHUNK_ROWS:, :] = jnp.concatenate([target, mask], axis=1).astype(BF16)


def whole(a):
    return pl.BlockSpec(a.shape, lambda g, w: (0,) * len(a.shape))


def block_of(turn, core):
    return core[0] if turn == 0 else 1 - core[0]


def forward_call(core, turn, pair4, weights, words=None, partial=None):
    steps = SIDE // F_COLS
    block = pl.BlockSpec((SIDE, 1, F_COLS, 128), lambda g, w: (0, block_of(turn, w), g, 0))
    in_specs = [block] + [whole(a) for a in weights]
    args = [pair4, *weights]
    alias = {}
    if turn == 1:
        in_specs.append(whole(words))
        args.append(words)
        in_specs.append(pl.BlockSpec(memory_space=pl.ANY))
        alias = {1 + len(args): 0}
        args.append(partial)
    outs = (
        jax.ShapeDtypeStruct(pair4.shape, BF16),
        jax.ShapeDtypeStruct((CHUNK_ROWS, 128), BF16),
        jax.ShapeDtypeStruct((CHUNK_ROWS + turn * SIDE, 128), BF16),
    )
    pairs = SIDE * SIDE

    def body(*refs):
        forward_body(turn, *refs)

    return pl.pallas_call(
        body,
        out_shape=outs,
        grid_spec=pltpu.PrefetchScalarGridSpec(
            num_scalar_prefetch=1,
            grid=(steps,),
            in_specs=in_specs,
            out_specs=(block, whole(outs[1]), whole(outs[2])),
            scratch_shapes=[pltpu.VMEM((SIDE * F_COLS, 128), F32)],
        ),
        input_output_aliases=alias,
        cost_estimate=pl.CostEstimate(
            flops=pairs * 2 * 128 * 512 * 3, transcendentals=pairs * 512, bytes_accessed=pairs * 640
        ),
        compiler_params=pltpu.CompilerParams(
            dimension_semantics=("arbitrary",), vmem_limit_bytes=16 * 1024 * 1024
        ),
        name="forward",
    )(core, *args)


def backward_body(turn, first, last, core, *refs):
    pair, pair_out, mirror_a, mirror_b, mirror_words, words = refs[:6]
    gain, bias, w_gate, w_up, w_out, head_t = refs[6:12]
    rest = list(refs[12:])
    earlier = None
    if not first:
        earlier, rest = rest[:4], rest[4:]
    if last:
        keep, send = rest[:2]
        rest = rest[2:]
    g_in, g_out, g_head, g_small, s_normed, s_grad_in, s_hidden, s_pair = rest
    sums = (g_in, g_out, g_head, g_small)
    hid = w_out.shape[0]
    step = pl.program_id(0)

    @pl.when(step == 0)
    def _():
        for k, ref in enumerate(sums):
            ref[...] = jnp.zeros_like(ref) if first else earlier[k][...]

    lane = lax.broadcasted_iota(jnp.int32, (ROWS, 128), 1)
    wanted = (jnp.bitwise_and(lane, 63) + 64).astype(F32)
    lane_row = lax.broadcasted_iota(jnp.int32, (128, 128), 0)
    lane_col = lax.broadcasted_iota(jnp.int32, (128, 128), 1)
    same = (lane_row // 64 == lane_col // 64).astype(F32).astype(BF16)
    sum_bins = jnp.concatenate([same, same], axis=0)
    head_two = head_square(head_t[...])
    head_four = jnp.concatenate([head_two, head_two], axis=0)
    own = block_words(words, lax.rem(core[0] + turn, 2))
    own = jnp.bitwise_and(own, 65535) + 64 * jnp.right_shift(own, 16)
    own = own.astype(F32).astype(BF16)
    if turn == 0:
        other = block_words(mirror_words, core[0])
        other = jnp.bitwise_and(other, 65535) + 64 * jnp.right_shift(other, 16)
        other = other.astype(F32).astype(BF16)
    else:
        other = mirror_words[...].astype(F32)
        other = (other[:, :SIDE] + 64.0 * other[:, SIDE:]).astype(BF16)
    early = step < CHUNK_ROWS // (B_GROUPS * ROWS)
    pick_n = lax.broadcasted_iota(jnp.int32, (SIDE, 512), 1)
    pick_k = lax.broadcasted_iota(jnp.int32, (SIDE, 512), 0)
    pick_base = pick_n // 128 + (GROUP // 2) * (jnp.bitwise_and(pick_n, 127) // 64)

    for grp in range(B_GROUPS):
        at = slice(grp * 2 * ROWS, (grp + 1) * 2 * ROWS)
        x_out = pair_out[grp * GROUP : (grp + 1) * GROUP].reshape(2 * ROWS, 128)
        both = jnp.concatenate([x_out[:ROWS], x_out[ROWS:]], axis=1)
        half = dot(both, head_two, NT).astype(BF16)
        rows = slice(grp * ROWS, (grp + 1) * ROWS)
        mirror = jnp.where(early, mirror_a[rows, :].astype(F32), mirror_b[rows, :].astype(F32))
        logits = half.astype(F32) + mirror
        expo = 0.5 * jnp.exp(logits)
        high = expo.astype(BF16)
        low = (expo - high.astype(F32)).astype(BF16)
        total = dot(jnp.concatenate([high, low], axis=1), sum_bins)
        log_total = jnp.log(total) + 0.6931471805599453
        soft = jnp.exp(logits - log_total)
        group = step * B_GROUPS + grp
        pick = (pick_k == pick_base + GROUP * group).astype(F32).astype(BF16)
        codes = []
        for spread in (dot(own, pick, TN), dot(other, pick)):
            codes.append(
                jnp.concatenate([spread[:, 128 * a : 128 * (a + 1)] for a in range(4)], axis=0)
            )
        grads = [
            (
                (jnp.where(c >= 63.5, soft, 0.0) - jnp.where(c == wanted, 1.0, 0.0)) * (1.0 / 1024)
            ).astype(BF16)
            for c in codes
        ]
        loss_part = jnp.where(codes[0] == wanted, log_total - logits, 0.0)
        grad_both = jnp.concatenate(grads, axis=1)
        g_head[...] += dot(grad_both, both, TN)
        grad_pair = dot(grad_both, head_four).astype(BF16)
        grad_pair = jnp.concatenate([grad_pair[:, :128], grad_pair[:, 128:]], axis=0)
        s_pair[at, :] = grad_pair

        x_in = pair[grp * GROUP : (grp + 1) * GROUP].reshape(2 * ROWS, 128)
        unit_rows, normed = normalize(x_in, gain[...], bias[...])
        s_normed[at, :] = normed
        gate_pre = dot(normed, w_gate[...])
        up_pre = dot(normed, w_up[...])
        grad_hidden = dot(grad_pair, w_out[...], NT)
        squashed = sigmoid(gate_pre)
        silu_val = gate_pre * squashed
        s_hidden[at, :] = (silu_val * up_pre).astype(BF16)
        slope = squashed * (1.0 + gate_pre * (1.0 - squashed))
        s_grad_in[at, :hid] = (grad_hidden * up_pre * slope).astype(BF16)
        s_grad_in[at, hid:] = (grad_hidden * silu_val).astype(BF16)
        grad_normed = dot(s_grad_in[at, :hid], w_gate[...], NT)
        grad_normed += dot(s_grad_in[at, hid:], w_up[...], NT)
        fold = lambda v: jnp.sum(v.reshape(-1, 8, 128), axis=0)
        g_small[0:8, :] += fold(grad_normed * unit_rows)
        g_small[8:16, :] += fold(grad_normed)
        g_small[16:24, :] += fold(loss_part)
    g_in[...] += dot(s_normed[...], s_grad_in[...], TN)
    g_out[...] += dot(s_pair[...], s_hidden[...], TN)

    if not last:
        return

    def put_in(ref):
        for k in range(8):
            ref[128 * k : 128 * (k + 1), :] = g_in[:, 128 * k : 128 * (k + 1)]

    def put_rest(ref):
        for k in range(4):
            ref[128 * k : 128 * (k + 1), :] = g_out[:, 128 * k : 128 * (k + 1)].T
        ref[512:576, :] = (
            g_head[0:64, 0:128]
            + g_head[64:128, 128:256]
            + g_head[128:192, 0:128]
            + g_head[192:256, 128:256]
        )
        small = [jnp.sum(g_small[8 * k : 8 * k + 8, :], axis=0, keepdims=True) for k in range(3)]
        ref[576:584, :] = jnp.concatenate(small + [jnp.zeros((5, 128), F32)], axis=0)
        ref[584:1024, :] = jnp.zeros((440, 128), F32)

    at_end = step == pl.num_programs(0) - 1

    @pl.when(jnp.logical_and(at_end, core[0] == 0))
    def _():
        put_in(keep)
        put_rest(send)

    @pl.when(jnp.logical_and(at_end, core[0] != 0))
    def _():
        put_in(send)
        put_rest(keep)


def backward_call(
    core, turn, pair4, pair_out4, mirror_a, mirror_b, mirror_words, words, weights, earlier, last
):
    wide, hid = 2 * weights[2].shape[1], weights[4].shape[0]
    steps = SIDE // (GROUP * B_GROUPS)
    block = pl.BlockSpec(
        (GROUP * B_GROUPS, 1, SIDE, 128), lambda g, w: (g, block_of(turn, w), 0, 0)
    )
    rows = ROWS * B_GROUPS
    half_way = CHUNK_ROWS // rows
    fixed = (words, *weights)
    in_specs = [
        block,
        block,
        pl.BlockSpec((rows, 128), lambda g, w: (jnp.minimum(g, half_way - 1), 0)),
        pl.BlockSpec((rows, 128), lambda g, w: (jnp.maximum(g - half_way, 0), 0)),
        pl.BlockSpec((SIDE, 128), lambda g, w: (turn * CHUNK_ROWS // SIDE, 0)),
    ]
    in_specs += [whole(a) for a in fixed]
    args = [pair4, pair_out4, mirror_a, mirror_b, mirror_words, *fixed]
    sums = [(128, wide), (128, hid), (256, 256), (24, 128)]
    if earlier is not None:
        in_specs += [whole(a) for a in earlier]
        args += list(earlier)
    outs = [jax.ShapeDtypeStruct(s, F32) for s in ([(1024, 128)] * 2 if last else sums)]
    scratch = [pltpu.VMEM(s, F32) for s in sums] if last else []
    scratch += [
        pltpu.VMEM((2 * rows, 128), BF16),
        pltpu.VMEM((2 * rows, wide), BF16),
        pltpu.VMEM((2 * rows, hid), BF16),
        pltpu.VMEM((2 * rows, 128), BF16),
    ]
    pairs = SIDE * SIDE

    def body(*refs):
        backward_body(turn, earlier is None, last, *refs)

    return pl.pallas_call(
        body,
        out_shape=tuple(outs),
        grid_spec=pltpu.PrefetchScalarGridSpec(
            num_scalar_prefetch=1,
            grid=(steps,),
            in_specs=in_specs,
            out_specs=tuple(whole(a) for a in outs),
            scratch_shapes=scratch,
        ),
        cost_estimate=pl.CostEstimate(
            flops=pairs * 2 * 128 * 512 * 8, transcendentals=pairs * 640, bytes_accessed=pairs * 640
        ),
        compiler_params=pltpu.CompilerParams(
            dimension_semantics=("arbitrary",), vmem_limit_bytes=28 * 1024 * 1024
        ),
        name="backward",
    )(core, *args)


def unpack_body(core, mine, other, d_gate, d_up, d_out, d_head, d_gain, d_bias, loss):
    def fill(lower, upper):
        for k in range(4):
            d_gate[:, 128 * k : 128 * (k + 1)] = lower[128 * k : 128 * (k + 1), :]
            d_up[:, 128 * k : 128 * (k + 1)] = lower[512 + 128 * k : 640 + 128 * k, :]
        d_out[...] = upper[0:512, :]
        d_head[...] = upper[512:576, :]
        d_gain[...] = upper[576:577, :]
        d_bias[...] = upper[577:578, :]
        loss[0, 0] = jnp.sum(upper[578:579, :]) * (1.0 / 1048576)

    @pl.when(core[0] == 0)
    def _():
        fill(mine, other)

    @pl.when(core[0] != 0)
    def _():
        fill(other, mine)


def unpack_call(core, mine, other):
    shapes = [(128, 512), (128, 512), (512, 128), (64, 128), (1, 128), (1, 128), (1, 1)]
    outs = tuple(jax.ShapeDtypeStruct(s, F32) for s in shapes)
    specs = [whole(a) for a in outs[:-1]] + [pl.BlockSpec(memory_space=pltpu.SMEM)]
    return pl.pallas_call(
        unpack_body,
        out_shape=outs,
        grid_spec=pltpu.PrefetchScalarGridSpec(
            num_scalar_prefetch=1,
            grid=(1,),
            in_specs=[whole(mine), whole(other)],
            out_specs=tuple(specs),
        ),
        compiler_params=pltpu.CompilerParams(vmem_limit_bytes=8 * 1024 * 1024),
        name="unpack",
    )(core, mine, other)


def shards(
    pair, ln_gain, ln_bias, gate_weight, up_weight, out_weight, head_weight, targets, pair_mask
):
    rows_tile, _, width = pair.shape
    core = lax.rem(lax.axis_index("row"), 2).astype(jnp.int32).reshape(1)

    words = targets + 65536 * pair_mask
    tile_words = lax.all_to_all(words, "col", split_axis=1, concat_axis=0, tiled=True)

    pair4 = pair.reshape(rows_tile, 2, SIDE, width)
    weights = (
        ln_gain.reshape(1, width),
        ln_bias.reshape(1, width),
        gate_weight,
        up_weight,
        out_weight,
        head_weight.T,
    )
    out4, *sent0 = forward_call(core, 0, pair4, weights)
    words0 = send_to_mirror(tile_words, 0, None)
    mirror0 = [send_to_mirror(v, 0, route) for v, route in zip(sent0, ROUTES[0])]
    out4, *sent1 = forward_call(core, 1, pair4, weights, tile_words, out4)
    mirror1 = [send_to_mirror(v, 1, route) for v, route in zip(sent1, ROUTES[1])]
    sums = backward_call(core, 0, pair4, out4, *mirror0, words0, tile_words, weights, None, False)
    keep, send = backward_call(
        core, 1, pair4, out4, *mirror1, mirror1[1], tile_words, weights, sums, True
    )
    sibling = [(d, device_at(chip_of(d)[0], 1 - chip_of(d)[1])) for d in range(128)]
    groups = [[d for d in range(128) if chip_of(d)[1] == k] for k in range(2)]
    both_cores = (keep + lax.ppermute(send, AXES, sibling)).reshape(64, 16, 128)
    pieces = lax.all_to_all(
        both_cores, AXES, split_axis=0, concat_axis=0, axis_index_groups=groups, tiled=True
    )
    mine = jnp.sum(pieces, axis=0, keepdims=True)
    mine = lax.all_to_all(
        jnp.broadcast_to(mine, pieces.shape),
        AXES,
        split_axis=0,
        concat_axis=0,
        axis_index_groups=groups,
        tiled=True,
    ).reshape(1024, 128)
    other = lax.ppermute(mine, AXES, sibling)
    d_gate, d_up, d_out, d_head, d_gain, d_bias, loss = unpack_call(core, mine, other)
    return (
        out4.reshape(pair.shape),
        loss.reshape(()),
        d_gain.reshape(width),
        d_bias.reshape(width),
        d_gate,
        d_up,
        d_out,
        d_head.T,
    )


def solution(mesh):
    placed = (
        P("row", "col", None),
        P(),
        P(),
        P(),
        P(),
        P(),
        P(),
        P(AXES, None),
        P(AXES, None),
    )
    return jax.shard_map(
        shards,
        mesh=mesh,
        in_specs=placed,
        out_specs=(P("row", "col", None), P(), P(), P(), P(), P(), P(), P()),
        check_vma=False,
    )
```

```python
import jax
import jax.numpy as jnp
from jax import lax
from jax.experimental import pallas as pl
from jax.experimental.pallas import tpu as pltpu
from jax.sharding import PartitionSpec as P


EPSILON = 1e-05
F32 = jnp.float32
BF16 = jnp.bfloat16
AXES = ("row", "col")

SIDE = 64
GROUP = 8
F_COLS = 16
B_GROUPS = 2
ROWS = SIDE * GROUP // 2
CHUNK_ROWS = SIDE * SIDE // 4

ROUTES = (((0, 0, 1), (0, 0, 3)), ((0, 2, 0), None))


def chip_of(device):
    r, c = divmod(device, 8)
    return (c // 2, (r % 8) // 2, (c % 2) * 2 + r // 8), r % 2


def device_at(chip, core):
    x, y, z = chip
    return ((z % 2) * 8 + y * 2 + core) * 8 + x * 2 + z // 2


def mirror_of(device, turn):
    r, c = divmod(device, 8)
    return (2 * c + (r + turn) % 2) * 8 + r // 2


def shifted(device, shift):
    chip, core = chip_of(device)
    return device_at(tuple((a + b) % 4 for a, b in zip(chip, shift)), core)


def send_to_mirror(value, turn, route):
    devices = range(128)
    if route is None:
        return lax.ppermute(value, AXES, [(d, mirror_of(d, turn)) for d in devices])
    value = lax.ppermute(value, AXES, [(d, shifted(d, route)) for d in devices])
    return lax.ppermute(value, AXES, [(shifted(d, route), mirror_of(d, turn)) for d in devices])


def dot(left, right, dims=((1,), (0,))):
    return lax.dot_general(left, right, (dims, ((), ())), preferred_element_type=F32)


NT = ((1,), (1,))
TN = ((0,), (0,))


def normalize(rows_in, gain, bias):
    values = rows_in.astype(F32)
    centered = values - jnp.mean(values, axis=-1, keepdims=True)
    variance = jnp.mean(centered * centered, axis=-1, keepdims=True)
    unit_rows = centered * lax.rsqrt(variance + EPSILON)
    scaled = unit_rows * gain + bias
    return scaled, scaled.astype(BF16)


def sigmoid(values):
    return 0.5 * jnp.tanh(0.5 * values) + 0.5


def head_square(head_t):
    blank = jnp.zeros_like(head_t)
    return jnp.concatenate(
        [
            jnp.concatenate([head_t, blank], axis=1),
            jnp.concatenate([blank, head_t], axis=1),
        ],
        axis=0,
    )


def block_words(words, block):
    tile = words[...]
    return jnp.where(block == 0, tile[:, :SIDE], tile[:, SIDE:])


def forward_body(turn, core, pair, gain, bias, w_gate, w_up, w_out, head_t, *rest):
    pair_out, send_a, send_b, wide = rest[-4:]
    words = rest[:-4]
    step = pl.program_id(0)
    rows_in = pair[...].reshape(SIDE * F_COLS, 128)
    count = 2
    size = SIDE * F_COLS // count
    for k in range(count):
        part = rows_in[k * size : (k + 1) * size]
        _, normed = normalize(part, gain[...], bias[...])
        gate_pre = dot(normed, w_gate[...])
        up_pre = dot(normed, w_up[...])
        hidden = (gate_pre * sigmoid(gate_pre) * up_pre).astype(BF16)
        result = (part.astype(F32) + dot(hidden, w_out[...])).astype(BF16)
        pair_out[k * size // F_COLS : (k + 1) * size // F_COLS] = result.reshape(
            size // F_COLS, 1, F_COLS, 128
        )
        wide[k * size : (k + 1) * size, :] = result.astype(F32)
    head_two = head_square(head_t[...])
    halves = []
    for grp in range(F_COLS // GROUP):
        left, right = [
            jnp.concatenate(
                [
                    wide[pl.ds(grp * GROUP + shift + a, SIDE, stride=F_COLS), :]
                    for a in range(GROUP // 2)
                ],
                axis=0,
            )
            for shift in (0, GROUP // 2)
        ]
        both = jnp.concatenate([left, right], axis=1).astype(BF16)
        halves.append(dot(both, head_two, NT).astype(BF16))
    rows = ROWS * F_COLS // GROUP
    per_chunk = CHUNK_ROWS // rows
    first_row = pl.multiple_of(lax.rem(step, per_chunk) * rows, rows)

    @pl.when(step < per_chunk)
    def _():
        send_a[pl.ds(first_row, rows), :] = jnp.concatenate(halves, axis=0)

    @pl.when(step >= per_chunk)
    def _():
        send_b[pl.ds(first_row, rows), :] = jnp.concatenate(halves, axis=0)

    if turn == 0:
        return

    @pl.when(step == 0)
    def _():
        own = block_words(words[0], lax.rem(core[0] + turn, 2))
        target = jnp.bitwise_and(own, 65535).astype(F32)
        mask = jnp.right_shift(own, 16).astype(F32)
        send_b[CHUNK_ROWS:, :] = jnp.concatenate([target, mask], axis=1).astype(BF16)


def whole(a):
    return pl.BlockSpec(a.shape, lambda g, w: (0,) * len(a.shape))


def block_of(turn, core):
    return core[0] if turn == 0 else 1 - core[0]


def forward_call(core, turn, pair4, weights, words=None, partial=None):
    steps = SIDE // F_COLS
    block = pl.BlockSpec((SIDE, 1, F_COLS, 128), lambda g, w: (0, block_of(turn, w), g, 0))
    in_specs = [block] + [whole(a) for a in weights]
    args = [pair4, *weights]
    alias = {}
    if turn == 1:
        in_specs.append(whole(words))
        args.append(words)
        in_specs.append(pl.BlockSpec(memory_space=pl.ANY))
        alias = {1 + len(args): 0}
        args.append(partial)
    outs = (
        jax.ShapeDtypeStruct(pair4.shape, BF16),
        jax.ShapeDtypeStruct((CHUNK_ROWS, 128), BF16),
        jax.ShapeDtypeStruct((CHUNK_ROWS + turn * SIDE, 128), BF16),
    )
    pairs = SIDE * SIDE

    def body(*refs):
        forward_body(turn, *refs)

    return pl.pallas_call(
        body,
        out_shape=outs,
        grid_spec=pltpu.PrefetchScalarGridSpec(
            num_scalar_prefetch=1,
            grid=(steps,),
            in_specs=in_specs,
            out_specs=(block, whole(outs[1]), whole(outs[2])),
            scratch_shapes=[pltpu.VMEM((SIDE * F_COLS, 128), F32)],
        ),
        input_output_aliases=alias,
        cost_estimate=pl.CostEstimate(
            flops=pairs * 2 * 128 * 512 * 3, transcendentals=pairs * 512, bytes_accessed=pairs * 640
        ),
        compiler_params=pltpu.CompilerParams(
            dimension_semantics=("arbitrary",), vmem_limit_bytes=16 * 1024 * 1024
        ),
        name="forward",
    )(core, *args)


def prepare_body(core, pair, gain, bias, w_gate, w_up, left, silu, up_slope, hidden):
    rows_in = pair[...].reshape(-1, 128)
    count = 2
    size = rows_in.shape[0] // count
    for k in range(count):
        at = slice(k * size, (k + 1) * size)
        scaled, normed = normalize(rows_in[at], gain[...], bias[...])
        left[at, :128] = normed
        left[at, 128:] = (normed.astype(F32) - scaled).astype(BF16)
        gate_pre = dot(normed, w_gate[...])
        up_pre = dot(normed, w_up[...])
        squashed = sigmoid(gate_pre)
        silu_val = gate_pre * squashed
        silu[at, :] = silu_val
        hidden[at, :] = (silu_val * up_pre).astype(BF16)
        up_slope[at, :] = up_pre * (squashed * (1.0 + gate_pre * (1.0 - squashed)))


def prepare_call(core, pair4, gain, bias, w_gate, w_up):
    hid = w_gate.shape[1]
    steps = SIDE // (GROUP * B_GROUPS)
    first = GROUP * B_GROUPS
    rows = first * SIDE
    pairs = 2 * SIDE * SIDE
    outs = (
        jax.ShapeDtypeStruct((pairs, 256), BF16),
        jax.ShapeDtypeStruct((pairs, hid), F32),
        jax.ShapeDtypeStruct((pairs, hid), F32),
        jax.ShapeDtypeStruct((pairs, hid), BF16),
    )
    args = (pair4, gain, bias, w_gate, w_up)
    return pl.pallas_call(
        prepare_body,
        out_shape=outs,
        grid_spec=pltpu.PrefetchScalarGridSpec(
            num_scalar_prefetch=1,
            grid=(2 * steps,),
            in_specs=[
                pl.BlockSpec(
                    (first, 1, SIDE, 128),
                    lambda g, w: (lax.rem(g, steps), lax.rem(w[0] + g // steps, 2), 0, 0),
                )
            ]
            + [whole(a) for a in args[1:]],
            out_specs=tuple(pl.BlockSpec((rows, a.shape[1]), lambda g, w: (g, 0)) for a in outs),
        ),
        cost_estimate=pl.CostEstimate(
            flops=pairs * 2 * 128 * 512 * 2, transcendentals=pairs * 512, bytes_accessed=pairs * 5888
        ),
        compiler_params=pltpu.CompilerParams(
            dimension_semantics=("arbitrary",), vmem_limit_bytes=28 * 1024 * 1024
        ),
        name="prepare",
    )(core, *args)


def backward_body(turn, first, last, core, *refs):
    left, silu, up_slope, hidden, pair_out, mirror_a, mirror_b, mirror_words, words = refs[:9]
    gain, bias, w_gate, w_up, w_out, head_t = refs[9:15]
    rest = list(refs[15:])
    earlier = None
    if not first:
        earlier, rest = rest[:5], rest[5:]
    if last:
        keep, send = rest[:2]
        rest = rest[2:]
    g_in, g_out, g_head, g_cols, g_loss, s_grad_in, s_pair = rest
    sums = (g_in, g_out, g_head, g_cols, g_loss)
    hid = w_out.shape[0]
    step = pl.program_id(0)

    @pl.when(step == 0)
    def _():
        for k, ref in enumerate(sums):
            ref[...] = jnp.zeros_like(ref) if first else earlier[k][...]

    lane = lax.broadcasted_iota(jnp.int32, (ROWS, 128), 1)
    wanted = (jnp.bitwise_and(lane, 63) + 64).astype(F32)
    lane_row = lax.broadcasted_iota(jnp.int32, (128, 128), 0)
    lane_col = lax.broadcasted_iota(jnp.int32, (128, 128), 1)
    same = (lane_row // 64 == lane_col // 64).astype(F32).astype(BF16)
    sum_bins = jnp.concatenate([same, same], axis=0)
    head_two = head_square(head_t[...])
    head_four = jnp.concatenate([head_two, head_two], axis=0)
    own = block_words(words, lax.rem(core[0] + turn, 2))
    own = jnp.bitwise_and(own, 65535) + 64 * jnp.right_shift(own, 16)
    own = own.astype(F32).astype(BF16)
    if turn == 0:
        other = block_words(mirror_words, core[0])
        other = jnp.bitwise_and(other, 65535) + 64 * jnp.right_shift(other, 16)
        other = other.astype(F32).astype(BF16)
    else:
        other = mirror_words[...].astype(F32)
        other = (other[:, :SIDE] + 64.0 * other[:, SIDE:]).astype(BF16)
    early = step < CHUNK_ROWS // (B_GROUPS * ROWS)
    pick_n = lax.broadcasted_iota(jnp.int32, (SIDE, 512), 1)
    pick_k = lax.broadcasted_iota(jnp.int32, (SIDE, 512), 0)
    pick_base = pick_n // 128 + (GROUP // 2) * (jnp.bitwise_and(pick_n, 127) // 64)

    for grp in range(B_GROUPS):
        at = slice(grp * 2 * ROWS, (grp + 1) * 2 * ROWS)
        x_out = pair_out[grp * GROUP : (grp + 1) * GROUP].reshape(2 * ROWS, 128)
        both = jnp.concatenate([x_out[:ROWS], x_out[ROWS:]], axis=1)
        half = dot(both, head_two, NT).astype(BF16)
        rows = slice(grp * ROWS, (grp + 1) * ROWS)
        mirror = jnp.where(early, mirror_a[rows, :].astype(F32), mirror_b[rows, :].astype(F32))
        logits = half.astype(F32) + mirror
        expo = 0.5 * jnp.exp(logits)
        high = expo.astype(BF16)
        low = (expo - high.astype(F32)).astype(BF16)
        total = dot(jnp.concatenate([high, low], axis=1), sum_bins)
        log_total = jnp.log(total) + 0.6931471805599453
        soft = jnp.exp(logits - log_total)
        group = step * B_GROUPS + grp
        pick = (pick_k == pick_base + GROUP * group).astype(F32).astype(BF16)
        codes = []
        for spread in (dot(own, pick, TN), dot(other, pick)):
            codes.append(
                jnp.concatenate([spread[:, 128 * a : 128 * (a + 1)] for a in range(4)], axis=0)
            )
        grads = [
            (
                (jnp.where(c >= 63.5, soft, 0.0) - jnp.where(c == wanted, 1.0, 0.0)) * (1.0 / 1024)
            ).astype(BF16)
            for c in codes
        ]
        loss_part = jnp.where(codes[0] == wanted, log_total - logits, 0.0)
        grad_both = jnp.concatenate(grads, axis=1)
        g_head[...] += dot(grad_both, both, TN)
        grad_pair = dot(grad_both, head_four).astype(BF16)
        grad_pair = jnp.concatenate([grad_pair[:, :128], grad_pair[:, 128:]], axis=0)
        s_pair[at, :] = grad_pair

        grad_hidden = dot(grad_pair, w_out[...], NT)
        fold = lambda v: jnp.sum(v.astype(F32).reshape(-1, 8, v.shape[1]), axis=0)
        grad_gate_pre = (grad_hidden * up_slope[at, :]).astype(BF16)
        grad_up_pre = (grad_hidden * silu[at, :]).astype(BF16)
        s_grad_in[at, :hid] = grad_gate_pre
        s_grad_in[at, hid:] = grad_up_pre
        g_cols[:, :hid] += fold(grad_gate_pre)
        g_cols[:, hid:] += fold(grad_up_pre)
        g_loss[...] += fold(loss_part)
    g_in[...] += dot(left[...], s_grad_in[...], TN)
    g_out[...] += dot(s_pair[...], hidden[...], TN)

    if not last:
        return

    def put_in(ref):
        for k in range(8):
            ref[128 * k : 128 * (k + 1), :] = g_in[0:128, 128 * k : 128 * (k + 1)]

    def put_rest(ref):
        for k in range(4):
            ref[128 * k : 128 * (k + 1), :] = g_out[:, 128 * k : 128 * (k + 1)].T
        ref[512:576, :] = (
            g_head[0:64, 0:128]
            + g_head[64:128, 128:256]
            + g_head[128:192, 0:128]
            + g_head[192:256, 128:256]
        )
        through, along = jnp.zeros((128, 128), F32), jnp.zeros((128, 128), F32)
        cols = jnp.sum(g_cols[...], axis=0, keepdims=True)
        for k in range(8):
            lanes = slice(128 * k, 128 * (k + 1))
            w = w_gate[:, lanes] if k < 4 else w_up[:, 128 * (k - 4) : 128 * (k - 3)]
            w = w.astype(F32)
            through += w * cols[:, lanes]
            along += w * (g_in[0:128, lanes] - g_in[128:256, lanes])
        d_bias = jnp.sum(through.T, axis=0, keepdims=True)
        d_gain = (jnp.sum(along.T, axis=0, keepdims=True) - bias[...] * d_bias) / gain[...]
        loss = jnp.sum(g_loss[...], axis=0, keepdims=True)
        ref[576:584, :] = jnp.concatenate([d_gain, d_bias, loss, jnp.zeros((5, 128), F32)], axis=0)
        ref[584:1024, :] = jnp.zeros((440, 128), F32)

    at_end = step == pl.num_programs(0) - 1

    @pl.when(jnp.logical_and(at_end, core[0] == 0))
    def _():
        put_in(keep)
        put_rest(send)

    @pl.when(jnp.logical_and(at_end, core[0] != 0))
    def _():
        put_in(send)
        put_rest(keep)


def backward_call(
    core, turn, ready, pair_out4, mirror_a, mirror_b, mirror_words, words, weights, earlier, last
):
    wide, hid = 2 * weights[2].shape[1], weights[4].shape[0]
    steps = SIDE // (GROUP * B_GROUPS)
    block = pl.BlockSpec(
        (GROUP * B_GROUPS, 1, SIDE, 128), lambda g, w: (g, block_of(turn, w), 0, 0)
    )
    rows = ROWS * B_GROUPS
    half_way = CHUNK_ROWS // rows
    wide_rows = lambda a: pl.BlockSpec((2 * rows, a.shape[1]), lambda g, w: (turn * steps + g, 0))
    fixed = (words, *weights)
    in_specs = [wide_rows(a) for a in ready] + [
        block,
        pl.BlockSpec((rows, 128), lambda g, w: (jnp.minimum(g, half_way - 1), 0)),
        pl.BlockSpec((rows, 128), lambda g, w: (jnp.maximum(g - half_way, 0), 0)),
        pl.BlockSpec((SIDE, 128), lambda g, w: (turn * CHUNK_ROWS // SIDE, 0)),
    ]
    in_specs += [whole(a) for a in fixed]
    args = [*ready, pair_out4, mirror_a, mirror_b, mirror_words, *fixed]
    sums = [(256, wide), (128, hid), (256, 256), (8, wide), (8, 128)]
    if earlier is not None:
        in_specs += [whole(a) for a in earlier]
        args += list(earlier)
    outs = [jax.ShapeDtypeStruct(s, F32) for s in ([(1024, 128)] * 2 if last else sums)]
    scratch = [pltpu.VMEM(s, F32) for s in sums] if last else []
    scratch += [
        pltpu.VMEM((2 * rows, wide), BF16),
        pltpu.VMEM((2 * rows, 128), BF16),
    ]
    pairs = SIDE * SIDE

    def body(*refs):
        backward_body(turn, earlier is None, last, *refs)

    return pl.pallas_call(
        body,
        out_shape=tuple(outs),
        grid_spec=pltpu.PrefetchScalarGridSpec(
            num_scalar_prefetch=1,
            grid=(steps,),
            in_specs=in_specs,
            out_specs=tuple(whole(a) for a in outs),
            scratch_shapes=scratch,
        ),
        cost_estimate=pl.CostEstimate(
            flops=pairs * 2 * 128 * 512 * 6,
            transcendentals=pairs * 192,
            bytes_accessed=pairs * 6400,
        ),
        compiler_params=pltpu.CompilerParams(
            dimension_semantics=("arbitrary",), vmem_limit_bytes=32 * 1024 * 1024
        ),
        name="backward",
    )(core, *args)


def unpack_body(core, mine, other, d_gate, d_up, d_out, d_head, d_gain, d_bias, loss):
    def fill(lower, upper):
        for k in range(4):
            d_gate[:, 128 * k : 128 * (k + 1)] = lower[128 * k : 128 * (k + 1), :]
            d_up[:, 128 * k : 128 * (k + 1)] = lower[512 + 128 * k : 640 + 128 * k, :]
        d_out[...] = upper[0:512, :]
        d_head[...] = upper[512:576, :]
        d_gain[...] = upper[576:577, :]
        d_bias[...] = upper[577:578, :]
        loss[0, 0] = jnp.sum(upper[578:579, :]) * (1.0 / 1048576)

    @pl.when(core[0] == 0)
    def _():
        fill(mine, other)

    @pl.when(core[0] != 0)
    def _():
        fill(other, mine)


def unpack_call(core, mine, other):
    shapes = [(128, 512), (128, 512), (512, 128), (64, 128), (1, 128), (1, 128), (1, 1)]
    outs = tuple(jax.ShapeDtypeStruct(s, F32) for s in shapes)
    specs = [whole(a) for a in outs[:-1]] + [pl.BlockSpec(memory_space=pltpu.SMEM)]
    return pl.pallas_call(
        unpack_body,
        out_shape=outs,
        grid_spec=pltpu.PrefetchScalarGridSpec(
            num_scalar_prefetch=1,
            grid=(1,),
            in_specs=[whole(mine), whole(other)],
            out_specs=tuple(specs),
        ),
        compiler_params=pltpu.CompilerParams(vmem_limit_bytes=8 * 1024 * 1024),
        name="unpack",
    )(core, mine, other)


def shards(
    pair, ln_gain, ln_bias, gate_weight, up_weight, out_weight, head_weight, targets, pair_mask
):
    rows_tile, _, width = pair.shape
    core = lax.rem(lax.axis_index("row"), 2).astype(jnp.int32).reshape(1)

    words = targets + 65536 * pair_mask
    tile_words = lax.all_to_all(words, "col", split_axis=1, concat_axis=0, tiled=True)

    pair4 = pair.reshape(rows_tile, 2, SIDE, width)
    weights = (
        ln_gain.reshape(1, width),
        ln_bias.reshape(1, width),
        gate_weight,
        up_weight,
        out_weight,
        head_weight.T,
    )
    in_hbm = lambda a: pltpu.with_memory_space_constraint(a, pltpu.HBM)
    out4, *sent0 = forward_call(core, 0, in_hbm(pair4), [in_hbm(a) for a in weights])
    words0 = send_to_mirror(tile_words, 0, None)
    mirror0 = [send_to_mirror(v, 0, route) for v, route in zip(sent0, ROUTES[0])]
    out4, *sent1 = forward_call(core, 1, pair4, weights, tile_words, out4)
    mirror1 = [send_to_mirror(v, 1, route) for v, route in zip(sent1, ROUTES[1])]
    held = in_hbm(out4)
    ready = prepare_call(core, pair4, *weights[:4])
    sums = backward_call(core, 0, ready, held, *mirror0, words0, tile_words, weights, None, False)
    keep, send = backward_call(
        core, 1, ready, held, *mirror1, mirror1[1], tile_words, weights, sums, True
    )
    sibling = [(d, device_at(chip_of(d)[0], 1 - chip_of(d)[1])) for d in range(128)]
    groups = [[d for d in range(128) if chip_of(d)[1] == k] for k in range(2)]
    both_cores = (keep + lax.ppermute(send, AXES, sibling)).reshape(64, 16, 128)
    pieces = lax.all_to_all(
        both_cores, AXES, split_axis=0, concat_axis=0, axis_index_groups=groups, tiled=True
    )
    mine = jnp.sum(pieces, axis=0, keepdims=True)
    mine = lax.all_to_all(
        jnp.broadcast_to(mine, pieces.shape),
        AXES,
        split_axis=0,
        concat_axis=0,
        axis_index_groups=groups,
        tiled=True,
    ).reshape(1024, 128)
    other = lax.ppermute(mine, AXES, sibling)
    d_gate, d_up, d_out, d_head, d_gain, d_bias, loss = unpack_call(core, mine, other)
    return (
        out4.reshape(pair.shape),
        loss.reshape(()),
        d_gain.reshape(width),
        d_bias.reshape(width),
        d_gate,
        d_up,
        d_out,
        d_head.T,
    )


def solution(mesh):
    placed = (
        P("row", "col", None),
        P(),
        P(),
        P(),
        P(),
        P(),
        P(),
        P(AXES, None),
        P(AXES, None),
    )
    return jax.shard_map(
        shards,
        mesh=mesh,
        in_specs=placed,
        out_specs=(P("row", "col", None), P(), P(), P(), P(), P(), P(), P()),
        check_vma=False,
    )
```

```python
import jax
import jax.numpy as jnp
from jax import lax
from jax.experimental import pallas as pl
from jax.experimental.pallas import tpu as pltpu
from jax.sharding import PartitionSpec as P


EPSILON = 1e-05
F32 = jnp.float32
BF16 = jnp.bfloat16
AXES = ("row", "col")

SIDE = 64
GROUP = 8
F_COLS = 32
B_GROUPS = 2
ROWS = SIDE * GROUP // 2
CHUNK_ROWS = SIDE * SIDE // 4

ROUTES = (((0, 0, 1), (0, 0, 3)), ((0, 2, 0), None))


def chip_of(device):
    r, c = divmod(device, 8)
    return (c // 2, (r % 8) // 2, (c % 2) * 2 + r // 8), r % 2


def device_at(chip, core):
    x, y, z = chip
    return ((z % 2) * 8 + y * 2 + core) * 8 + x * 2 + z // 2


def mirror_of(device, turn):
    r, c = divmod(device, 8)
    return (2 * c + (r + turn) % 2) * 8 + r // 2


def shifted(device, shift):
    chip, core = chip_of(device)
    return device_at(tuple((a + b) % 4 for a, b in zip(chip, shift)), core)


def send_to_mirror(value, turn, route):
    devices = range(128)
    if route is None:
        return lax.ppermute(value, AXES, [(d, mirror_of(d, turn)) for d in devices])
    value = lax.ppermute(value, AXES, [(d, shifted(d, route)) for d in devices])
    return lax.ppermute(value, AXES, [(shifted(d, route), mirror_of(d, turn)) for d in devices])


def dot(left, right, dims=((1,), (0,))):
    return lax.dot_general(left, right, (dims, ((), ())), preferred_element_type=F32)


NT = ((1,), (1,))
TN = ((0,), (0,))


def normalize(rows_in, gain, bias):
    values = rows_in.astype(F32)
    centered = values - jnp.mean(values, axis=-1, keepdims=True)
    variance = jnp.mean(centered * centered, axis=-1, keepdims=True)
    unit_rows = centered * lax.rsqrt(variance + EPSILON)
    return unit_rows, (unit_rows * gain + bias).astype(BF16)


def sigmoid(values):
    return 0.5 * jnp.tanh(0.5 * values) + 0.5


def head_square(head_t):
    blank = jnp.zeros_like(head_t)
    return jnp.concatenate(
        [
            jnp.concatenate([head_t, blank], axis=1),
            jnp.concatenate([blank, head_t], axis=1),
        ],
        axis=0,
    )


def block_words(words, block):
    tile = words[...]
    return jnp.where(block == 0, tile[:, :SIDE], tile[:, SIDE:])


def forward_body(turn, core, pair, gain, bias, w_gate, w_up, w_out, head_t, *rest):
    pair_out, send_a, send_b, wide = rest[-4:]
    words = rest[:-4]
    step = pl.program_id(0)
    rows_in = pair[...].reshape(SIDE * F_COLS, 128)
    count = 4
    size = SIDE * F_COLS // count
    for k in range(count):
        part = rows_in[k * size : (k + 1) * size]
        _, normed = normalize(part, gain[...], bias[...])
        gate_pre = dot(normed, w_gate[...])
        up_pre = dot(normed, w_up[...])
        hidden = (gate_pre * sigmoid(gate_pre) * up_pre).astype(BF16)
        result = (part.astype(F32) + dot(hidden, w_out[...])).astype(BF16)
        pair_out[k * size // F_COLS : (k + 1) * size // F_COLS] = result.reshape(
            size // F_COLS, 1, F_COLS, 128
        )
        wide[k * size : (k + 1) * size, :] = result.astype(F32)
    head_two = head_square(head_t[...])
    halves = []
    for grp in range(F_COLS // GROUP):
        left, right = [
            jnp.concatenate(
                [
                    wide[pl.ds(grp * GROUP + shift + a, SIDE, stride=F_COLS), :]
                    for a in range(GROUP // 2)
                ],
                axis=0,
            )
            for shift in (0, GROUP // 2)
        ]
        both = jnp.concatenate([left, right], axis=1).astype(BF16)
        halves.append(dot(both, head_two, NT).astype(BF16))
    rows = ROWS * F_COLS // GROUP
    per_chunk = CHUNK_ROWS // rows
    first_row = pl.multiple_of(lax.rem(step, per_chunk) * rows, rows)

    @pl.when(step < per_chunk)
    def _():
        send_a[pl.ds(first_row, rows), :] = jnp.concatenate(halves, axis=0)

    @pl.when(step >= per_chunk)
    def _():
        send_b[pl.ds(first_row, rows), :] = jnp.concatenate(halves, axis=0)

    if turn == 0:
        return

    @pl.when(step == 0)
    def _():
        own = block_words(words[0], lax.rem(core[0] + turn, 2))
        target = jnp.bitwise_and(own, 65535).astype(F32)
        mask = jnp.right_shift(own, 16).astype(F32)
        send_b[CHUNK_ROWS:, :] = jnp.concatenate([target, mask], axis=1).astype(BF16)


def whole(a):
    return pl.BlockSpec(a.shape, lambda g, w: (0,) * len(a.shape))


def block_of(turn, core):
    return core[0] if turn == 0 else 1 - core[0]


def forward_call(core, turn, pair4, weights, words=None, partial=None):
    steps = SIDE // F_COLS
    block = pl.BlockSpec((SIDE, 1, F_COLS, 128), lambda g, w: (0, block_of(turn, w), g, 0))
    in_specs = [block] + [whole(a) for a in weights]
    args = [pair4, *weights]
    alias = {}
    if turn == 1:
        in_specs.append(whole(words))
        args.append(words)
        in_specs.append(pl.BlockSpec(memory_space=pl.ANY))
        alias = {1 + len(args): 0}
        args.append(partial)
    outs = (
        jax.ShapeDtypeStruct(pair4.shape, BF16),
        jax.ShapeDtypeStruct((CHUNK_ROWS, 128), BF16),
        jax.ShapeDtypeStruct((CHUNK_ROWS + turn * SIDE, 128), BF16),
    )
    pairs = SIDE * SIDE

    def body(*refs):
        forward_body(turn, *refs)

    return pl.pallas_call(
        body,
        out_shape=outs,
        grid_spec=pltpu.PrefetchScalarGridSpec(
            num_scalar_prefetch=1,
            grid=(steps,),
            in_specs=in_specs,
            out_specs=(block, whole(outs[1]), whole(outs[2])),
            scratch_shapes=[pltpu.VMEM((SIDE * F_COLS, 128), F32)],
        ),
        input_output_aliases=alias,
        cost_estimate=pl.CostEstimate(
            flops=pairs * 2 * 128 * 512 * 3, transcendentals=pairs * 512, bytes_accessed=pairs * 640
        ),
        compiler_params=pltpu.CompilerParams(
            dimension_semantics=("arbitrary",), vmem_limit_bytes=16 * 1024 * 1024
        ),
        name="forward",
    )(core, *args)


def backward_body(turn, first, last, core, *refs):
    pair, pair_out, mirror_a, mirror_b, mirror_words, words = refs[:6]
    gain, bias, w_gate, w_up, w_out, head_t = refs[6:12]
    rest = list(refs[12:])
    earlier = None
    if not first:
        earlier, rest = rest[:4], rest[4:]
    if last:
        keep, send = rest[:2]
        rest = rest[2:]
    g_in, g_out, g_head, g_small, s_normed, s_grad_in, s_hidden, s_pair = rest
    sums = (g_in, g_out, g_head, g_small)
    hid = w_out.shape[0]
    step = pl.program_id(0)

    @pl.when(step == 0)
    def _():
        for k, ref in enumerate(sums):
            ref[...] = jnp.zeros_like(ref) if first else earlier[k][...]

    lane = lax.broadcasted_iota(jnp.int32, (ROWS, 128), 1)
    wanted = (jnp.bitwise_and(lane, 63) + 64).astype(F32)
    lane_row = lax.broadcasted_iota(jnp.int32, (128, 128), 0)
    lane_col = lax.broadcasted_iota(jnp.int32, (128, 128), 1)
    same = (lane_row // 64 == lane_col // 64).astype(F32).astype(BF16)
    sum_bins = jnp.concatenate([same, same], axis=0)
    head_two = head_square(head_t[...])
    head_four = jnp.concatenate([head_two, head_two], axis=0)
    own = block_words(words, lax.rem(core[0] + turn, 2))
    own = jnp.bitwise_and(own, 65535) + 64 * jnp.right_shift(own, 16)
    own = own.astype(F32).astype(BF16)
    if turn == 0:
        other = block_words(mirror_words, core[0])
        other = jnp.bitwise_and(other, 65535) + 64 * jnp.right_shift(other, 16)
        other = other.astype(F32).astype(BF16)
    else:
        other = mirror_words[...].astype(F32)
        other = (other[:, :SIDE] + 64.0 * other[:, SIDE:]).astype(BF16)
    early = step < CHUNK_ROWS // (B_GROUPS * ROWS)
    pick_n = lax.broadcasted_iota(jnp.int32, (SIDE, 512), 1)
    pick_k = lax.broadcasted_iota(jnp.int32, (SIDE, 512), 0)
    pick_base = pick_n // 128 + (GROUP // 2) * (jnp.bitwise_and(pick_n, 127) // 64)

    for grp in range(B_GROUPS):
        at = slice(grp * 2 * ROWS, (grp + 1) * 2 * ROWS)
        x_out = pair_out[grp * GROUP : (grp + 1) * GROUP].reshape(2 * ROWS, 128)
        both = jnp.concatenate([x_out[:ROWS], x_out[ROWS:]], axis=1)
        half = dot(both, head_two, NT).astype(BF16)
        rows = slice(grp * ROWS, (grp + 1) * ROWS)
        mirror = jnp.where(early, mirror_a[rows, :].astype(F32), mirror_b[rows, :].astype(F32))
        logits = half.astype(F32) + mirror
        expo = 0.5 * jnp.exp(logits)
        high = expo.astype(BF16)
        low = (expo - high.astype(F32)).astype(BF16)
        total = dot(jnp.concatenate([high, low], axis=1), sum_bins)
        log_total = jnp.log(total) + 0.6931471805599453
        soft = jnp.exp(logits - log_total)
        group = step * B_GROUPS + grp
        pick = (pick_k == pick_base + GROUP * group).astype(F32).astype(BF16)
        codes = []
        for spread in (dot(own, pick, TN), dot(other, pick)):
            codes.append(
                jnp.concatenate([spread[:, 128 * a : 128 * (a + 1)] for a in range(4)], axis=0)
            )
        grads = [
            (
                (jnp.where(c >= 63.5, soft, 0.0) - jnp.where(c == wanted, 1.0, 0.0)) * (1.0 / 1024)
            ).astype(BF16)
            for c in codes
        ]
        loss_part = jnp.where(codes[0] == wanted, log_total - logits, 0.0)
        grad_both = jnp.concatenate(grads, axis=1)
        g_head[...] += dot(grad_both, both, TN)
        grad_pair = dot(grad_both, head_four).astype(BF16)
        grad_pair = jnp.concatenate([grad_pair[:, :128], grad_pair[:, 128:]], axis=0)
        s_pair[at, :] = grad_pair

        x_in = pair[grp * GROUP : (grp + 1) * GROUP].reshape(2 * ROWS, 128)
        unit_rows, normed = normalize(x_in, gain[...], bias[...])
        s_normed[at, :] = normed
        gate_pre = dot(normed, w_gate[...])
        up_pre = dot(normed, w_up[...])
        grad_hidden = dot(grad_pair, w_out[...], NT)
        squashed = sigmoid(gate_pre)
        silu_val = gate_pre * squashed
        s_hidden[at, :] = (silu_val * up_pre).astype(BF16)
        slope = squashed * (1.0 + gate_pre * (1.0 - squashed))
        s_grad_in[at, :hid] = (grad_hidden * up_pre * slope).astype(BF16)
        s_grad_in[at, hid:] = (grad_hidden * silu_val).astype(BF16)
        grad_normed = dot(s_grad_in[at, :hid], w_gate[...], NT)
        grad_normed += dot(s_grad_in[at, hid:], w_up[...], NT)
        fold = lambda v: jnp.sum(v.reshape(-1, 8, 128), axis=0)
        g_small[0:8, :] += fold(grad_normed * unit_rows)
        g_small[8:16, :] += fold(grad_normed)
        g_small[16:24, :] += fold(loss_part)
    g_in[...] += dot(s_normed[...], s_grad_in[...], TN)
    g_out[...] += dot(s_pair[...], s_hidden[...], TN)

    if not last:
        return

    def put_in(ref):
        for k in range(8):
            ref[128 * k : 128 * (k + 1), :] = g_in[:, 128 * k : 128 * (k + 1)]

    def put_rest(ref):
        for k in range(4):
            ref[128 * k : 128 * (k + 1), :] = g_out[:, 128 * k : 128 * (k + 1)].T
        ref[512:576, :] = (
            g_head[0:64, 0:128]
            + g_head[64:128, 128:256]
            + g_head[128:192, 0:128]
            + g_head[192:256, 128:256]
        )
        small = [jnp.sum(g_small[8 * k : 8 * k + 8, :], axis=0, keepdims=True) for k in range(3)]
        ref[576:584, :] = jnp.concatenate(small + [jnp.zeros((5, 128), F32)], axis=0)
        ref[584:1024, :] = jnp.zeros((440, 128), F32)

    at_end = step == pl.num_programs(0) - 1

    @pl.when(jnp.logical_and(at_end, core[0] == 0))
    def _():
        put_in(keep)
        put_rest(send)

    @pl.when(jnp.logical_and(at_end, core[0] != 0))
    def _():
        put_in(send)
        put_rest(keep)


def backward_call(
    core, turn, pair4, pair_out4, mirror_a, mirror_b, mirror_words, words, weights, earlier, last
):
    wide, hid = 2 * weights[2].shape[1], weights[4].shape[0]
    steps = SIDE // (GROUP * B_GROUPS)
    block = pl.BlockSpec(
        (GROUP * B_GROUPS, 1, SIDE, 128), lambda g, w: (g, block_of(turn, w), 0, 0)
    )
    rows = ROWS * B_GROUPS
    half_way = CHUNK_ROWS // rows
    fixed = (words, *weights)
    in_specs = [
        block,
        block,
        pl.BlockSpec((rows, 128), lambda g, w: (jnp.minimum(g, half_way - 1), 0)),
        pl.BlockSpec((rows, 128), lambda g, w: (jnp.maximum(g - half_way, 0), 0)),
        pl.BlockSpec((SIDE, 128), lambda g, w: (turn * CHUNK_ROWS // SIDE, 0)),
    ]
    in_specs += [whole(a) for a in fixed]
    args = [pair4, pair_out4, mirror_a, mirror_b, mirror_words, *fixed]
    sums = [(128, wide), (128, hid), (256, 256), (24, 128)]
    if earlier is not None:
        in_specs += [whole(a) for a in earlier]
        args += list(earlier)
    outs = [jax.ShapeDtypeStruct(s, F32) for s in ([(1024, 128)] * 2 if last else sums)]
    scratch = [pltpu.VMEM(s, F32) for s in sums] if last else []
    scratch += [
        pltpu.VMEM((2 * rows, 128), BF16),
        pltpu.VMEM((2 * rows, wide), BF16),
        pltpu.VMEM((2 * rows, hid), BF16),
        pltpu.VMEM((2 * rows, 128), BF16),
    ]
    pairs = SIDE * SIDE

    def body(*refs):
        backward_body(turn, earlier is None, last, *refs)

    return pl.pallas_call(
        body,
        out_shape=tuple(outs),
        grid_spec=pltpu.PrefetchScalarGridSpec(
            num_scalar_prefetch=1,
            grid=(steps,),
            in_specs=in_specs,
            out_specs=tuple(whole(a) for a in outs),
            scratch_shapes=scratch,
        ),
        cost_estimate=pl.CostEstimate(
            flops=pairs * 2 * 128 * 512 * 8, transcendentals=pairs * 640, bytes_accessed=pairs * 640
        ),
        compiler_params=pltpu.CompilerParams(
            dimension_semantics=("arbitrary",), vmem_limit_bytes=28 * 1024 * 1024
        ),
        name="backward",
    )(core, *args)


def unpack_body(core, mine, other, d_gate, d_up, d_out, d_head, d_gain, d_bias, loss):
    def fill(lower, upper):
        for k in range(4):
            d_gate[:, 128 * k : 128 * (k + 1)] = lower[128 * k : 128 * (k + 1), :]
            d_up[:, 128 * k : 128 * (k + 1)] = lower[512 + 128 * k : 640 + 128 * k, :]
        d_out[...] = upper[0:512, :]
        d_head[...] = upper[512:576, :]
        d_gain[...] = upper[576:577, :]
        d_bias[...] = upper[577:578, :]
        loss[0, 0] = jnp.sum(upper[578:579, :]) * (1.0 / 1048576)

    @pl.when(core[0] == 0)
    def _():
        fill(mine, other)

    @pl.when(core[0] != 0)
    def _():
        fill(other, mine)


def unpack_call(core, mine, other):
    shapes = [(128, 512), (128, 512), (512, 128), (64, 128), (1, 128), (1, 128), (1, 1)]
    outs = tuple(jax.ShapeDtypeStruct(s, F32) for s in shapes)
    specs = [whole(a) for a in outs[:-1]] + [pl.BlockSpec(memory_space=pltpu.SMEM)]
    return pl.pallas_call(
        unpack_body,
        out_shape=outs,
        grid_spec=pltpu.PrefetchScalarGridSpec(
            num_scalar_prefetch=1,
            grid=(1,),
            in_specs=[whole(mine), whole(other)],
            out_specs=tuple(specs),
        ),
        compiler_params=pltpu.CompilerParams(vmem_limit_bytes=8 * 1024 * 1024),
        name="unpack",
    )(core, mine, other)


def shards(
    pair, ln_gain, ln_bias, gate_weight, up_weight, out_weight, head_weight, targets, pair_mask
):
    rows_tile, _, width = pair.shape
    core = lax.rem(lax.axis_index("row"), 2).astype(jnp.int32).reshape(1)

    words = targets + 65536 * pair_mask
    tile_words = lax.all_to_all(words, "col", split_axis=1, concat_axis=0, tiled=True)

    pair4 = pair.reshape(rows_tile, 2, SIDE, width)
    weights = (
        ln_gain.reshape(1, width),
        ln_bias.reshape(1, width),
        gate_weight,
        up_weight,
        out_weight,
        head_weight.T,
    )
    in_hbm = lambda a: pltpu.with_memory_space_constraint(a, pltpu.HBM)
    out4, *sent0 = forward_call(core, 0, in_hbm(pair4), [in_hbm(a) for a in weights])
    words0 = send_to_mirror(tile_words, 0, None)
    mirror0 = [send_to_mirror(v, 0, route) for v, route in zip(sent0, ROUTES[0])]
    out4, *sent1 = forward_call(core, 1, pair4, weights, tile_words, out4)
    mirror1 = [send_to_mirror(v, 1, route) for v, route in zip(sent1, ROUTES[1])]
    held = in_hbm(out4)
    sums = backward_call(core, 0, pair4, held, *mirror0, words0, tile_words, weights, None, False)
    keep, send = backward_call(
        core, 1, pair4, held, *mirror1, mirror1[1], tile_words, weights, sums, True
    )
    sibling = [(d, device_at(chip_of(d)[0], 1 - chip_of(d)[1])) for d in range(128)]
    groups = [[d for d in range(128) if chip_of(d)[1] == k] for k in range(2)]
    both_cores = (keep + lax.ppermute(send, AXES, sibling)).reshape(64, 16, 128)
    pieces = lax.all_to_all(
        both_cores, AXES, split_axis=0, concat_axis=0, axis_index_groups=groups, tiled=True
    )
    mine = jnp.sum(pieces, axis=0, keepdims=True)
    mine = lax.all_to_all(
        jnp.broadcast_to(mine, pieces.shape),
        AXES,
        split_axis=0,
        concat_axis=0,
        axis_index_groups=groups,
        tiled=True,
    ).reshape(1024, 128)
    other = lax.ppermute(mine, AXES, sibling)
    d_gate, d_up, d_out, d_head, d_gain, d_bias, loss = unpack_call(core, mine, other)
    return (
        out4.reshape(pair.shape),
        loss.reshape(()),
        d_gain.reshape(width),
        d_bias.reshape(width),
        d_gate,
        d_up,
        d_out,
        d_head.T,
    )


def solution(mesh):
    placed = (
        P("row", "col", None),
        P(),
        P(),
        P(),
        P(),
        P(),
        P(),
        P(AXES, None),
        P(AXES, None),
    )
    return jax.shard_map(
        shards,
        mesh=mesh,
        in_specs=placed,
        out_specs=(P("row", "col", None), P(), P(), P(), P(), P(), P(), P()),
        check_vma=False,
    )
```

```python
import jax
import jax.numpy as jnp
from jax import lax
from jax.experimental import pallas as pl
from jax.experimental.pallas import tpu as pltpu
from jax.sharding import PartitionSpec as P


EPSILON = 1e-05
F32 = jnp.float32
BF16 = jnp.bfloat16
AXES = ("row", "col")

SIDE = 64
GROUP = 8
F_COLS = 32
B_GROUPS = 2
ROWS = SIDE * GROUP // 2
CHUNK_ROWS = SIDE * SIDE // 4

ROUTES = (((0, 1, 1), (0, 3, 3)), ((0, 2, 2), None))


def chip_of(device):
    r, c = divmod(device, 8)
    return (c // 2, (r % 8) // 2, (c % 2) * 2 + r // 8), r % 2


def device_at(chip, core):
    x, y, z = chip
    return ((z % 2) * 8 + y * 2 + core) * 8 + x * 2 + z // 2


def mirror_of(device, turn):
    r, c = divmod(device, 8)
    return (2 * c + (r + turn) % 2) * 8 + r // 2


def shifted(device, shift):
    chip, core = chip_of(device)
    return device_at(tuple((a + b) % 4 for a, b in zip(chip, shift)), core)


def send_to_mirror(value, turn, route):
    devices = range(128)
    if route is None:
        return lax.ppermute(value, AXES, [(d, mirror_of(d, turn)) for d in devices])
    value = lax.ppermute(value, AXES, [(d, shifted(d, route)) for d in devices])
    return lax.ppermute(value, AXES, [(shifted(d, route), mirror_of(d, turn)) for d in devices])


def dot(left, right, dims=((1,), (0,))):
    return lax.dot_general(left, right, (dims, ((), ())), preferred_element_type=F32)


NT = ((1,), (1,))
TN = ((0,), (0,))


def normalize(rows_in, gain, bias):
    values = rows_in.astype(F32)
    centered = values - jnp.mean(values, axis=-1, keepdims=True)
    variance = jnp.mean(centered * centered, axis=-1, keepdims=True)
    unit_rows = centered * lax.rsqrt(variance + EPSILON)
    return unit_rows, (unit_rows * gain + bias).astype(BF16)


def sigmoid(values):
    return 0.5 * jnp.tanh(0.5 * values) + 0.5


def head_square(head_t):
    blank = jnp.zeros_like(head_t)
    return jnp.concatenate(
        [
            jnp.concatenate([head_t, blank], axis=1),
            jnp.concatenate([blank, head_t], axis=1),
        ],
        axis=0,
    )


def block_words(words, block):
    tile = words[...]
    return jnp.where(block == 0, tile[:, :SIDE], tile[:, SIDE:])


def forward_body(chunks, core, pair, gain, bias, w_gate, w_up, w_out, head_t, *rest):
    pair_out, *sends = rest[-2 - len(chunks) : -1]
    wide = rest[-1]
    rows_in = pair[...].reshape(SIDE * F_COLS, 128)
    count = 4
    size = SIDE * F_COLS // count
    for k in range(count):
        part = rows_in[k * size : (k + 1) * size]
        _, normed = normalize(part, gain[...], bias[...])
        gate_pre = dot(normed, w_gate[...])
        up_pre = dot(normed, w_up[...])
        hidden = (gate_pre * sigmoid(gate_pre) * up_pre).astype(BF16)
        result = (part.astype(F32) + dot(hidden, w_out[...])).astype(BF16)
        pair_out[k * size // F_COLS : (k + 1) * size // F_COLS] = result.reshape(
            size // F_COLS, 1, F_COLS, 128
        )
        wide[k * size : (k + 1) * size, :] = result.astype(F32)
    head_two = head_square(head_t[...])
    halves = []
    for grp in range(F_COLS // GROUP):
        left, right = [
            jnp.concatenate(
                [
                    wide[pl.ds(grp * GROUP + shift + a, SIDE, stride=F_COLS), :]
                    for a in range(GROUP // 2)
                ],
                axis=0,
            )
            for shift in (0, GROUP // 2)
        ]
        both = jnp.concatenate([left, right], axis=1).astype(BF16)
        halves.append(dot(both, head_two, NT).astype(BF16))
    for k, chunk in enumerate(chunks):

        @pl.when(pl.program_id(0) == k)
        def _():
            sends[k][:CHUNK_ROWS, :] = jnp.concatenate(halves, axis=0)
            if chunk == 3:
                own = block_words(rest[0], lax.rem(core[0] + 1, 2))
                target = jnp.bitwise_and(own, 65535).astype(F32)
                mask = jnp.right_shift(own, 16).astype(F32)
                both = jnp.concatenate([target, mask], axis=1)
                sends[k][CHUNK_ROWS:, :] = both.astype(BF16)


def whole(a):
    return pl.BlockSpec(a.shape, lambda g, w: (0,) * len(a.shape))


def block_of(turn, core):
    return core[0] if turn == 0 else 1 - core[0]


def forward_call(core, chunks, pair4, weights, words=None, partial=None):
    block = pl.BlockSpec(
        (SIDE, 1, F_COLS, 128),
        lambda g, w: (
            0,
            lax.rem(w[0] + (g + chunks[0]) // 2, 2),
            lax.rem(g + chunks[0], 2),
            0,
        ),
    )
    in_specs = [block] + [whole(a) for a in weights]
    args = [pair4, *weights]
    alias = {}
    if words is not None:
        in_specs.append(whole(words))
        args.append(words)
    if partial is not None:
        in_specs.append(pl.BlockSpec(memory_space=pl.ANY))
        alias = {1 + len(args): 0}
        args.append(partial)
    sizes = [CHUNK_ROWS + (SIDE if chunk == 3 else 0) for chunk in chunks]
    outs = (jax.ShapeDtypeStruct(pair4.shape, BF16),) + tuple(
        jax.ShapeDtypeStruct((size, 128), BF16) for size in sizes
    )
    pairs = SIDE * F_COLS * len(chunks)

    def body(*refs):
        forward_body(chunks, *refs)

    return pl.pallas_call(
        body,
        out_shape=outs,
        grid_spec=pltpu.PrefetchScalarGridSpec(
            num_scalar_prefetch=1,
            grid=(len(chunks),),
            in_specs=in_specs,
            out_specs=(block,) + tuple(whole(a) for a in outs[1:]),
            scratch_shapes=[pltpu.VMEM((SIDE * F_COLS, 128), F32)],
        ),
        input_output_aliases=alias,
        cost_estimate=pl.CostEstimate(
            flops=pairs * 2 * 128 * 512 * 3, transcendentals=pairs * 512, bytes_accessed=pairs * 640
        ),
        compiler_params=pltpu.CompilerParams(
            dimension_semantics=("arbitrary",), vmem_limit_bytes=20 * 1024 * 1024
        ),
        name="forward",
    )(core, *args)


def backward_body(turn, first, last, core, *refs):
    pair, pair_out, mirror_a, mirror_b, mirror_words, words = refs[:6]
    gain, bias, w_gate, w_up, w_out, head_t = refs[6:12]
    rest = list(refs[12:])
    earlier = None
    if not first:
        earlier, rest = rest[:4], rest[4:]
    if last:
        keep, send = rest[:2]
        rest = rest[2:]
    g_in, g_out, g_head, g_small, s_normed, s_grad_in, s_hidden, s_pair = rest
    sums = (g_in, g_out, g_head, g_small)
    hid = w_out.shape[0]
    step = pl.program_id(0)

    @pl.when(step == 0)
    def _():
        for k, ref in enumerate(sums):
            ref[...] = jnp.zeros_like(ref) if first else earlier[k][...]

    lane = lax.broadcasted_iota(jnp.int32, (ROWS, 128), 1)
    wanted = (jnp.bitwise_and(lane, 63) + 64).astype(F32)
    lane_row = lax.broadcasted_iota(jnp.int32, (128, 128), 0)
    lane_col = lax.broadcasted_iota(jnp.int32, (128, 128), 1)
    same = (lane_row // 64 == lane_col // 64).astype(F32).astype(BF16)
    sum_bins = jnp.concatenate([same, same], axis=0)
    head_two = head_square(head_t[...])
    head_four = jnp.concatenate([head_two, head_two], axis=0)
    own = block_words(words, lax.rem(core[0] + turn, 2))
    own = jnp.bitwise_and(own, 65535) + 64 * jnp.right_shift(own, 16)
    own = own.astype(F32).astype(BF16)
    if turn == 0:
        other = block_words(mirror_words, core[0])
        other = jnp.bitwise_and(other, 65535) + 64 * jnp.right_shift(other, 16)
        other = other.astype(F32).astype(BF16)
    else:
        other = mirror_words[...].astype(F32)
        other = (other[:, :SIDE] + 64.0 * other[:, SIDE:]).astype(BF16)
    early = step < CHUNK_ROWS // (B_GROUPS * ROWS)
    pick_n = lax.broadcasted_iota(jnp.int32, (SIDE, 512), 1)
    pick_k = lax.broadcasted_iota(jnp.int32, (SIDE, 512), 0)
    pick_base = pick_n // 128 + (GROUP // 2) * (jnp.bitwise_and(pick_n, 127) // 64)

    for grp in range(B_GROUPS):
        at = slice(grp * 2 * ROWS, (grp + 1) * 2 * ROWS)
        x_out = pair_out[grp * GROUP : (grp + 1) * GROUP].reshape(2 * ROWS, 128)
        both = jnp.concatenate([x_out[:ROWS], x_out[ROWS:]], axis=1)
        half = dot(both, head_two, NT).astype(BF16)
        rows = slice(grp * ROWS, (grp + 1) * ROWS)
        mirror = jnp.where(early, mirror_a[rows, :].astype(F32), mirror_b[rows, :].astype(F32))
        logits = half.astype(F32) + mirror
        expo = 0.5 * jnp.exp(logits)
        high = expo.astype(BF16)
        low = (expo - high.astype(F32)).astype(BF16)
        total = dot(jnp.concatenate([high, low], axis=1), sum_bins)
        log_total = jnp.log(total) + 0.6931471805599453
        soft = jnp.exp(logits - log_total)
        group = step * B_GROUPS + grp
        pick = (pick_k == pick_base + GROUP * group).astype(F32).astype(BF16)
        codes = []
        for spread in (dot(own, pick, TN), dot(other, pick)):
            codes.append(
                jnp.concatenate([spread[:, 128 * a : 128 * (a + 1)] for a in range(4)], axis=0)
            )
        grads = [
            (
                (jnp.where(c >= 63.5, soft, 0.0) - jnp.where(c == wanted, 1.0, 0.0)) * (1.0 / 1024)
            ).astype(BF16)
            for c in codes
        ]
        loss_part = jnp.where(codes[0] == wanted, log_total - logits, 0.0)
        grad_both = jnp.concatenate(grads, axis=1)
        g_head[...] += dot(grad_both, both, TN)
        grad_pair = dot(grad_both, head_four).astype(BF16)
        grad_pair = jnp.concatenate([grad_pair[:, :128], grad_pair[:, 128:]], axis=0)
        s_pair[at, :] = grad_pair

        x_in = pair[grp * GROUP : (grp + 1) * GROUP].reshape(2 * ROWS, 128)
        unit_rows, normed = normalize(x_in, gain[...], bias[...])
        s_normed[at, :] = normed
        gate_pre = dot(normed, w_gate[...])
        up_pre = dot(normed, w_up[...])
        grad_hidden = dot(grad_pair, w_out[...], NT)
        squashed = sigmoid(gate_pre)
        silu_val = gate_pre * squashed
        s_hidden[at, :] = (silu_val * up_pre).astype(BF16)
        slope = squashed * (1.0 + gate_pre * (1.0 - squashed))
        s_grad_in[at, :hid] = (grad_hidden * up_pre * slope).astype(BF16)
        s_grad_in[at, hid:] = (grad_hidden * silu_val).astype(BF16)
        grad_normed = dot(s_grad_in[at, :hid], w_gate[...], NT)
        grad_normed += dot(s_grad_in[at, hid:], w_up[...], NT)
        fold = lambda v: jnp.sum(v.reshape(-1, 8, 128), axis=0)
        g_small[0:8, :] += fold(grad_normed * unit_rows)
        g_small[8:16, :] += fold(grad_normed)
        g_small[16:24, :] += fold(loss_part)
    g_in[...] += dot(s_normed[...], s_grad_in[...], TN)
    g_out[...] += dot(s_pair[...], s_hidden[...], TN)

    if not last:
        return

    def put_in(ref):
        for k in range(8):
            ref[128 * k : 128 * (k + 1), :] = g_in[:, 128 * k : 128 * (k + 1)]

    def put_rest(ref):
        for k in range(4):
            ref[128 * k : 128 * (k + 1), :] = g_out[:, 128 * k : 128 * (k + 1)].T
        ref[512:576, :] = (
            g_head[0:64, 0:128]
            + g_head[64:128, 128:256]
            + g_head[128:192, 0:128]
            + g_head[192:256, 128:256]
        )
        small = [jnp.sum(g_small[8 * k : 8 * k + 8, :], axis=0, keepdims=True) for k in range(3)]
        ref[576:584, :] = jnp.concatenate(small + [jnp.zeros((5, 128), F32)], axis=0)
        ref[584:1024, :] = jnp.zeros((440, 128), F32)

    at_end = step == pl.num_programs(0) - 1

    @pl.when(jnp.logical_and(at_end, core[0] == 0))
    def _():
        put_in(keep)
        put_rest(send)

    @pl.when(jnp.logical_and(at_end, core[0] != 0))
    def _():
        put_in(send)
        put_rest(keep)


def backward_call(
    core, turn, pair4, pair_out4, mirror_a, mirror_b, mirror_words, words, weights, earlier, last
):
    wide, hid = 2 * weights[2].shape[1], weights[4].shape[0]
    steps = SIDE // (GROUP * B_GROUPS)
    block = pl.BlockSpec(
        (GROUP * B_GROUPS, 1, SIDE, 128), lambda g, w: (g, block_of(turn, w), 0, 0)
    )
    rows = ROWS * B_GROUPS
    half_way = CHUNK_ROWS // rows
    fixed = (words, *weights)
    in_specs = [
        block,
        block,
        pl.BlockSpec((rows, 128), lambda g, w: (jnp.minimum(g, half_way - 1), 0)),
        pl.BlockSpec((rows, 128), lambda g, w: (jnp.maximum(g - half_way, 0), 0)),
        pl.BlockSpec((SIDE, 128), lambda g, w: (turn * CHUNK_ROWS // SIDE, 0)),
    ]
    in_specs += [whole(a) for a in fixed]
    args = [pair4, pair_out4, mirror_a, mirror_b, mirror_words, *fixed]
    sums = [(128, wide), (128, hid), (256, 256), (24, 128)]
    if earlier is not None:
        in_specs += [whole(a) for a in earlier]
        args += list(earlier)
    outs = [jax.ShapeDtypeStruct(s, F32) for s in ([(1024, 128)] * 2 if last else sums)]
    scratch = [pltpu.VMEM(s, F32) for s in sums] if last else []
    scratch += [
        pltpu.VMEM((2 * rows, 128), BF16),
        pltpu.VMEM((2 * rows, wide), BF16),
        pltpu.VMEM((2 * rows, hid), BF16),
        pltpu.VMEM((2 * rows, 128), BF16),
    ]
    pairs = SIDE * SIDE

    def body(*refs):
        backward_body(turn, earlier is None, last, *refs)

    return pl.pallas_call(
        body,
        out_shape=tuple(outs),
        grid_spec=pltpu.PrefetchScalarGridSpec(
            num_scalar_prefetch=1,
            grid=(steps,),
            in_specs=in_specs,
            out_specs=tuple(whole(a) for a in outs),
            scratch_shapes=scratch,
        ),
        cost_estimate=pl.CostEstimate(
            flops=pairs * 2 * 128 * 512 * 8, transcendentals=pairs * 640, bytes_accessed=pairs * 640
        ),
        compiler_params=pltpu.CompilerParams(
            dimension_semantics=("arbitrary",), vmem_limit_bytes=28 * 1024 * 1024
        ),
        name="backward",
    )(core, *args)


def unpack_body(core, mine, other, d_gate, d_up, d_out, d_head, d_gain, d_bias, loss):
    def fill(lower, upper):
        for k in range(4):
            d_gate[:, 128 * k : 128 * (k + 1)] = lower[128 * k : 128 * (k + 1), :]
            d_up[:, 128 * k : 128 * (k + 1)] = lower[512 + 128 * k : 640 + 128 * k, :]
        d_out[...] = upper[0:512, :]
        d_head[...] = upper[512:576, :]
        d_gain[...] = upper[576:577, :]
        d_bias[...] = upper[577:578, :]
        loss[0, 0] = jnp.sum(upper[578:579, :]) * (1.0 / 1048576)

    @pl.when(core[0] == 0)
    def _():
        fill(mine, other)

    @pl.when(core[0] != 0)
    def _():
        fill(other, mine)


def unpack_call(core, mine, other):
    shapes = [(128, 512), (128, 512), (512, 128), (64, 128), (1, 128), (1, 128), (1, 1)]
    outs = tuple(jax.ShapeDtypeStruct(s, F32) for s in shapes)
    specs = [whole(a) for a in outs[:-1]] + [pl.BlockSpec(memory_space=pltpu.SMEM)]
    return pl.pallas_call(
        unpack_body,
        out_shape=outs,
        grid_spec=pltpu.PrefetchScalarGridSpec(
            num_scalar_prefetch=1,
            grid=(1,),
            in_specs=[whole(mine), whole(other)],
            out_specs=tuple(specs),
        ),
        compiler_params=pltpu.CompilerParams(vmem_limit_bytes=8 * 1024 * 1024),
        name="unpack",
    )(core, mine, other)


def shards(
    pair, ln_gain, ln_bias, gate_weight, up_weight, out_weight, head_weight, targets, pair_mask
):
    rows_tile, _, width = pair.shape
    core = lax.rem(lax.axis_index("row"), 2).astype(jnp.int32).reshape(1)

    words = targets + 65536 * pair_mask
    tile_words = lax.all_to_all(words, "col", split_axis=1, concat_axis=0, tiled=True)

    pair4 = pair.reshape(rows_tile, 2, SIDE, width)
    weights = (
        ln_gain.reshape(1, width),
        ln_bias.reshape(1, width),
        gate_weight,
        up_weight,
        out_weight,
        head_weight.T,
    )
    in_hbm = lambda a: pltpu.with_memory_space_constraint(a, pltpu.HBM)
    out4, *sent = forward_call(core, (0, 1, 2), in_hbm(pair4), [in_hbm(a) for a in weights])
    words0 = send_to_mirror(tile_words, 0, None)
    out4, last = forward_call(core, (3,), pair4, weights, tile_words, out4)
    mirror = [send_to_mirror(v, k // 2, ROUTES[k // 2][k % 2]) for k, v in enumerate((*sent, last))]
    mirror0, mirror1 = mirror[:2], mirror[2:]
    held = in_hbm(out4)
    sums = backward_call(core, 0, pair4, held, *mirror0, words0, tile_words, weights, None, False)
    keep, send = backward_call(
        core, 1, pair4, held, *mirror1, mirror1[1], tile_words, weights, sums, True
    )
    sibling = [(d, device_at(chip_of(d)[0], 1 - chip_of(d)[1])) for d in range(128)]
    groups = [[d for d in range(128) if chip_of(d)[1] == k] for k in range(2)]
    both_cores = (keep + lax.ppermute(send, AXES, sibling)).reshape(64, 16, 128)
    pieces = lax.all_to_all(
        both_cores, AXES, split_axis=0, concat_axis=0, axis_index_groups=groups, tiled=True
    )
    mine = jnp.sum(pieces, axis=0, keepdims=True)
    mine = lax.all_to_all(
        jnp.broadcast_to(mine, pieces.shape),
        AXES,
        split_axis=0,
        concat_axis=0,
        axis_index_groups=groups,
        tiled=True,
    ).reshape(1024, 128)
    other = lax.ppermute(mine, AXES, sibling)
    d_gate, d_up, d_out, d_head, d_gain, d_bias, loss = unpack_call(core, mine, other)
    return (
        out4.reshape(pair.shape),
        loss.reshape(()),
        d_gain.reshape(width),
        d_bias.reshape(width),
        d_gate,
        d_up,
        d_out,
        d_head.T,
    )


def solution(mesh):
    placed = (
        P("row", "col", None),
        P(),
        P(),
        P(),
        P(),
        P(),
        P(),
        P(AXES, None),
        P(AXES, None),
    )
    return jax.shard_map(
        shards,
        mesh=mesh,
        in_specs=placed,
        out_specs=(P("row", "col", None), P(), P(), P(), P(), P(), P(), P()),
        check_vma=False,
    )
```

```python
import jax
import jax.numpy as jnp
from jax import lax
from jax.experimental import pallas as pl
from jax.experimental.pallas import tpu as pltpu
from jax.sharding import PartitionSpec as P


EPSILON = 1e-05
F32 = jnp.float32
BF16 = jnp.bfloat16
AXES = ("row", "col")

SIDE = 64
GROUP = 8
F_COLS = 32
B_GROUPS = 2
ROWS = SIDE * GROUP // 2
CHUNK_ROWS = SIDE * SIDE // 4

ROUTES = (((0, 1, 1), (0, 3, 3)), ((0, 2, 2), None))


def chip_of(device):
    r, c = divmod(device, 8)
    return (c // 2, (r % 8) // 2, (c % 2) * 2 + r // 8), r % 2


def device_at(chip, core):
    x, y, z = chip
    return ((z % 2) * 8 + y * 2 + core) * 8 + x * 2 + z // 2


def mirror_of(device, turn):
    r, c = divmod(device, 8)
    return (2 * c + (r + turn) % 2) * 8 + r // 2


def shifted(device, shift):
    chip, core = chip_of(device)
    return device_at(tuple((a + b) % 4 for a, b in zip(chip, shift)), core)


def send_to_mirror(value, turn, route):
    devices = range(128)
    if route is None:
        return lax.ppermute(value, AXES, [(d, mirror_of(d, turn)) for d in devices])
    value = lax.ppermute(value, AXES, [(d, shifted(d, route)) for d in devices])
    return lax.ppermute(value, AXES, [(shifted(d, route), mirror_of(d, turn)) for d in devices])


def dot(left, right, dims=((1,), (0,))):
    return lax.dot_general(left, right, (dims, ((), ())), preferred_element_type=F32)


NT = ((1,), (1,))
TN = ((0,), (0,))


def normalize(rows_in, gain, bias):
    values = rows_in.astype(F32)
    centered = values - jnp.mean(values, axis=-1, keepdims=True)
    variance = jnp.mean(centered * centered, axis=-1, keepdims=True)
    unit_rows = centered * lax.rsqrt(variance + EPSILON)
    return unit_rows, (unit_rows * gain + bias).astype(BF16)


def sigmoid(values):
    return 0.5 * jnp.tanh(0.5 * values) + 0.5


def head_square(head_t):
    blank = jnp.zeros_like(head_t)
    return jnp.concatenate(
        [
            jnp.concatenate([head_t, blank], axis=1),
            jnp.concatenate([blank, head_t], axis=1),
        ],
        axis=0,
    )


def block_words(words, block):
    tile = words[...]
    return jnp.where(block == 0, tile[:, :SIDE], tile[:, SIDE:])


def forward_body(chunks, core, pair, gain, bias, w_gate, w_up, w_out, head_t, *rest):
    pair_out, *sends = rest[-2 - len(chunks) : -1]
    wide = rest[-1]
    rows_in = pair[...].reshape(SIDE * F_COLS, 128)
    count = 4
    size = SIDE * F_COLS // count
    for k in range(count):
        part = rows_in[k * size : (k + 1) * size]
        _, normed = normalize(part, gain[...], bias[...])
        gate_pre = dot(normed, w_gate[...])
        up_pre = dot(normed, w_up[...])
        hidden = (gate_pre * sigmoid(gate_pre) * up_pre).astype(BF16)
        result = (part.astype(F32) + dot(hidden, w_out[...])).astype(BF16)
        pair_out[k * size // F_COLS : (k + 1) * size // F_COLS] = result.reshape(
            size // F_COLS, 1, F_COLS, 128
        )
        wide[k * size : (k + 1) * size, :] = result.astype(F32)
    head_two = head_square(head_t[...])
    halves = []
    for grp in range(F_COLS // GROUP):
        left, right = [
            jnp.concatenate(
                [
                    wide[pl.ds(grp * GROUP + shift + a, SIDE, stride=F_COLS), :]
                    for a in range(GROUP // 2)
                ],
                axis=0,
            )
            for shift in (0, GROUP // 2)
        ]
        both = jnp.concatenate([left, right], axis=1).astype(BF16)
        halves.append(dot(both, head_two, NT).astype(BF16))
    for k in range(len(chunks)):

        @pl.when(pl.program_id(0) == k)
        def _():
            sends[k][...] = jnp.concatenate(halves, axis=0)


def whole(a):
    return pl.BlockSpec(a.shape, lambda g, w: (0,) * len(a.shape))


def block_of(turn, core):
    return core[0] if turn == 0 else 1 - core[0]


def forward_call(core, chunks, pair4, weights):
    block = pl.BlockSpec(
        (SIDE, 1, F_COLS, 128),
        lambda g, w: (
            0,
            lax.rem(w[0] + (g + chunks[0]) // 2, 2),
            lax.rem(g + chunks[0], 2),
            0,
        ),
    )
    in_specs = [block] + [whole(a) for a in weights]
    args = [pair4, *weights]
    outs = (jax.ShapeDtypeStruct(pair4.shape, BF16),) + tuple(
        jax.ShapeDtypeStruct((CHUNK_ROWS, 128), BF16) for _ in chunks
    )
    pairs = SIDE * F_COLS * len(chunks)

    def body(*refs):
        forward_body(chunks, *refs)

    return pl.pallas_call(
        body,
        out_shape=outs,
        grid_spec=pltpu.PrefetchScalarGridSpec(
            num_scalar_prefetch=1,
            grid=(len(chunks),),
            in_specs=in_specs,
            out_specs=(block,) + tuple(whole(a) for a in outs[1:]),
            scratch_shapes=[pltpu.VMEM((SIDE * F_COLS, 128), F32)],
        ),
        cost_estimate=pl.CostEstimate(
            flops=pairs * 2 * 128 * 512 * 3, transcendentals=pairs * 512, bytes_accessed=pairs * 640
        ),
        compiler_params=pltpu.CompilerParams(
            dimension_semantics=("arbitrary",), vmem_limit_bytes=24 * 1024 * 1024
        ),
        name="forward",
    )(core, *args)


def backward_body(turn, first, last, core, *refs):
    pair, pair_out, mirror_a, mirror_b, mirror_words, words = refs[:6]
    gain, bias, w_gate, w_up, w_out, head_t = refs[6:12]
    rest = list(refs[12:])
    earlier = None
    if not first:
        earlier, rest = rest[:4], rest[4:]
    if last:
        keep, send = rest[:2]
        rest = rest[2:]
    g_in, g_out, g_head, g_small, s_normed, s_grad_in, s_hidden, s_pair = rest
    sums = (g_in, g_out, g_head, g_small)
    hid = w_out.shape[0]
    step = pl.program_id(0)

    @pl.when(step == 0)
    def _():
        for k, ref in enumerate(sums):
            ref[...] = jnp.zeros_like(ref) if first else earlier[k][...]

    lane = lax.broadcasted_iota(jnp.int32, (ROWS, 128), 1)
    wanted = (jnp.bitwise_and(lane, 63) + 64).astype(F32)
    lane_row = lax.broadcasted_iota(jnp.int32, (128, 128), 0)
    lane_col = lax.broadcasted_iota(jnp.int32, (128, 128), 1)
    same = (lane_row // 64 == lane_col // 64).astype(F32).astype(BF16)
    sum_bins = jnp.concatenate([same, same], axis=0)
    head_two = head_square(head_t[...])
    head_four = jnp.concatenate([head_two, head_two], axis=0)
    own = block_words(words, lax.rem(core[0] + turn, 2))
    own = jnp.bitwise_and(own, 65535) + 64 * jnp.right_shift(own, 16)
    own = own.astype(F32).astype(BF16)
    other = block_words(mirror_words, core[0])
    other = jnp.bitwise_and(other, 65535) + 64 * jnp.right_shift(other, 16)
    other = other.astype(F32).astype(BF16)
    early = step < CHUNK_ROWS // (B_GROUPS * ROWS)
    pick_n = lax.broadcasted_iota(jnp.int32, (SIDE, 512), 1)
    pick_k = lax.broadcasted_iota(jnp.int32, (SIDE, 512), 0)
    pick_base = pick_n // 128 + (GROUP // 2) * (jnp.bitwise_and(pick_n, 127) // 64)

    for grp in range(B_GROUPS):
        at = slice(grp * 2 * ROWS, (grp + 1) * 2 * ROWS)
        x_out = pair_out[grp * GROUP : (grp + 1) * GROUP].reshape(2 * ROWS, 128)
        both = jnp.concatenate([x_out[:ROWS], x_out[ROWS:]], axis=1)
        half = dot(both, head_two, NT).astype(BF16)
        rows = slice(grp * ROWS, (grp + 1) * ROWS)
        mirror = jnp.where(early, mirror_a[rows, :].astype(F32), mirror_b[rows, :].astype(F32))
        logits = half.astype(F32) + mirror
        expo = 0.5 * jnp.exp(logits)
        high = expo.astype(BF16)
        low = (expo - high.astype(F32)).astype(BF16)
        total = dot(jnp.concatenate([high, low], axis=1), sum_bins)
        log_total = jnp.log(total) + 0.6931471805599453
        soft = jnp.exp(logits - log_total)
        group = step * B_GROUPS + grp
        pick = (pick_k == pick_base + GROUP * group).astype(F32).astype(BF16)
        codes = []
        for spread in (dot(own, pick, TN), dot(other, pick)):
            codes.append(
                jnp.concatenate([spread[:, 128 * a : 128 * (a + 1)] for a in range(4)], axis=0)
            )
        grads = [
            (
                (jnp.where(c >= 63.5, soft, 0.0) - jnp.where(c == wanted, 1.0, 0.0)) * (1.0 / 1024)
            ).astype(BF16)
            for c in codes
        ]
        loss_part = jnp.where(codes[0] == wanted, log_total - logits, 0.0)
        grad_both = jnp.concatenate(grads, axis=1)
        g_head[...] += dot(grad_both, both, TN)
        grad_pair = dot(grad_both, head_four).astype(BF16)
        grad_pair = jnp.concatenate([grad_pair[:, :128], grad_pair[:, 128:]], axis=0)
        s_pair[at, :] = grad_pair

        x_in = pair[grp * GROUP : (grp + 1) * GROUP].reshape(2 * ROWS, 128)
        unit_rows, normed = normalize(x_in, gain[...], bias[...])
        s_normed[at, :] = normed
        gate_pre = dot(normed, w_gate[...])
        up_pre = dot(normed, w_up[...])
        grad_hidden = dot(grad_pair, w_out[...], NT)
        squashed = sigmoid(gate_pre)
        silu_val = gate_pre * squashed
        s_hidden[at, :] = (silu_val * up_pre).astype(BF16)
        slope = squashed * (1.0 + gate_pre * (1.0 - squashed))
        s_grad_in[at, :hid] = (grad_hidden * up_pre * slope).astype(BF16)
        s_grad_in[at, hid:] = (grad_hidden * silu_val).astype(BF16)
        grad_normed = dot(s_grad_in[at, :hid], w_gate[...], NT)
        grad_normed += dot(s_grad_in[at, hid:], w_up[...], NT)
        fold = lambda v: jnp.sum(v.reshape(-1, 8, 128), axis=0)
        g_small[0:8, :] += fold(grad_normed * unit_rows)
        g_small[8:16, :] += fold(grad_normed)
        g_small[16:24, :] += fold(loss_part)
    g_in[...] += dot(s_normed[...], s_grad_in[...], TN)
    g_out[...] += dot(s_pair[...], s_hidden[...], TN)

    if not last:
        return

    def put_in(ref):
        for k in range(8):
            ref[128 * k : 128 * (k + 1), :] = g_in[:, 128 * k : 128 * (k + 1)]

    def put_rest(ref):
        for k in range(4):
            ref[128 * k : 128 * (k + 1), :] = g_out[:, 128 * k : 128 * (k + 1)].T
        ref[512:576, :] = (
            g_head[0:64, 0:128]
            + g_head[64:128, 128:256]
            + g_head[128:192, 0:128]
            + g_head[192:256, 128:256]
        )
        small = [jnp.sum(g_small[8 * k : 8 * k + 8, :], axis=0, keepdims=True) for k in range(3)]
        ref[576:584, :] = jnp.concatenate(small + [jnp.zeros((5, 128), F32)], axis=0)
        ref[584:1024, :] = jnp.zeros((440, 128), F32)

    at_end = step == pl.num_programs(0) - 1

    @pl.when(jnp.logical_and(at_end, core[0] == 0))
    def _():
        put_in(keep)
        put_rest(send)

    @pl.when(jnp.logical_and(at_end, core[0] != 0))
    def _():
        put_in(send)
        put_rest(keep)


def backward_call(
    core, turn, pair4, pair_out4, mirror_a, mirror_b, mirror_words, words, weights, earlier, last
):
    wide, hid = 2 * weights[2].shape[1], weights[4].shape[0]
    steps = SIDE // (GROUP * B_GROUPS)
    block = pl.BlockSpec(
        (GROUP * B_GROUPS, 1, SIDE, 128), lambda g, w: (g, block_of(turn, w), 0, 0)
    )
    rows = ROWS * B_GROUPS
    half_way = CHUNK_ROWS // rows
    fixed = (words, *weights)
    in_specs = [
        block,
        block,
        pl.BlockSpec((rows, 128), lambda g, w: (jnp.minimum(g, half_way - 1), 0)),
        pl.BlockSpec((rows, 128), lambda g, w: (jnp.maximum(g - half_way, 0), 0)),
        pl.BlockSpec((SIDE, 128), lambda g, w: (0, 0)),
    ]
    in_specs += [whole(a) for a in fixed]
    args = [pair4, pair_out4, mirror_a, mirror_b, mirror_words, *fixed]
    sums = [(128, wide), (128, hid), (256, 256), (24, 128)]
    if earlier is not None:
        in_specs += [whole(a) for a in earlier]
        args += list(earlier)
    outs = [jax.ShapeDtypeStruct(s, F32) for s in ([(1024, 128)] * 2 if last else sums)]
    scratch = [pltpu.VMEM(s, F32) for s in sums] if last else []
    scratch += [
        pltpu.VMEM((2 * rows, 128), BF16),
        pltpu.VMEM((2 * rows, wide), BF16),
        pltpu.VMEM((2 * rows, hid), BF16),
        pltpu.VMEM((2 * rows, 128), BF16),
    ]
    pairs = SIDE * SIDE

    def body(*refs):
        backward_body(turn, earlier is None, last, *refs)

    return pl.pallas_call(
        body,
        out_shape=tuple(outs),
        grid_spec=pltpu.PrefetchScalarGridSpec(
            num_scalar_prefetch=1,
            grid=(steps,),
            in_specs=in_specs,
            out_specs=tuple(whole(a) for a in outs),
            scratch_shapes=scratch,
        ),
        cost_estimate=pl.CostEstimate(
            flops=pairs * 2 * 128 * 512 * 8, transcendentals=pairs * 640, bytes_accessed=pairs * 640
        ),
        compiler_params=pltpu.CompilerParams(
            dimension_semantics=("arbitrary",), vmem_limit_bytes=28 * 1024 * 1024
        ),
        name="backward",
    )(core, *args)


def unpack_body(core, mine, other, d_gate, d_up, d_out, d_head, d_gain, d_bias, loss):
    def fill(lower, upper):
        for k in range(4):
            d_gate[:, 128 * k : 128 * (k + 1)] = lower[128 * k : 128 * (k + 1), :]
            d_up[:, 128 * k : 128 * (k + 1)] = lower[512 + 128 * k : 640 + 128 * k, :]
        d_out[...] = upper[0:512, :]
        d_head[...] = upper[512:576, :]
        d_gain[...] = upper[576:577, :]
        d_bias[...] = upper[577:578, :]
        loss[0, 0] = jnp.sum(upper[578:579, :]) * (1.0 / 1048576)

    @pl.when(core[0] == 0)
    def _():
        fill(mine, other)

    @pl.when(core[0] != 0)
    def _():
        fill(other, mine)


def unpack_call(core, mine, other):
    shapes = [(128, 512), (128, 512), (512, 128), (64, 128), (1, 128), (1, 128), (1, 1)]
    outs = tuple(jax.ShapeDtypeStruct(s, F32) for s in shapes)
    specs = [whole(a) for a in outs[:-1]] + [pl.BlockSpec(memory_space=pltpu.SMEM)]
    return pl.pallas_call(
        unpack_body,
        out_shape=outs,
        grid_spec=pltpu.PrefetchScalarGridSpec(
            num_scalar_prefetch=1,
            grid=(1,),
            in_specs=[whole(mine), whole(other)],
            out_specs=tuple(specs),
        ),
        compiler_params=pltpu.CompilerParams(vmem_limit_bytes=8 * 1024 * 1024),
        name="unpack",
    )(core, mine, other)


def shards(
    pair, ln_gain, ln_bias, gate_weight, up_weight, out_weight, head_weight, targets, pair_mask
):
    rows_tile, _, width = pair.shape
    core = lax.rem(lax.axis_index("row"), 2).astype(jnp.int32).reshape(1)

    words = targets + 65536 * pair_mask
    tile_words = lax.all_to_all(words, "col", split_axis=1, concat_axis=0, tiled=True)

    pair4 = pair.reshape(rows_tile, 2, SIDE, width)
    weights = (
        ln_gain.reshape(1, width),
        ln_bias.reshape(1, width),
        gate_weight,
        up_weight,
        out_weight,
        head_weight.T,
    )
    in_hbm = lambda a: pltpu.with_memory_space_constraint(a, pltpu.HBM)
    out4, *sent = forward_call(
        core, (0, 1, 2, 3), in_hbm(pair4), [in_hbm(a) for a in weights]
    )
    mirror = [send_to_mirror(v, k // 2, ROUTES[k // 2][k % 2]) for k, v in enumerate(sent)]
    mirror0, mirror1 = mirror[:2], mirror[2:]
    words0, words1 = [send_to_mirror(tile_words, k, None) for k in range(2)]
    held = in_hbm(out4)
    sums = backward_call(core, 0, pair4, held, *mirror0, words0, tile_words, weights, None, False)
    keep, send = backward_call(
        core, 1, pair4, held, *mirror1, words1, tile_words, weights, sums, True
    )
    sibling = [(d, device_at(chip_of(d)[0], 1 - chip_of(d)[1])) for d in range(128)]
    groups = [[d for d in range(128) if chip_of(d)[1] == k] for k in range(2)]
    both_cores = (keep + lax.ppermute(send, AXES, sibling)).reshape(64, 16, 128)
    pieces = lax.all_to_all(
        both_cores, AXES, split_axis=0, concat_axis=0, axis_index_groups=groups, tiled=True
    )
    mine = jnp.sum(pieces, axis=0, keepdims=True)
    mine = lax.all_to_all(
        jnp.broadcast_to(mine, pieces.shape),
        AXES,
        split_axis=0,
        concat_axis=0,
        axis_index_groups=groups,
        tiled=True,
    ).reshape(1024, 128)
    other = lax.ppermute(mine, AXES, sibling)
    d_gate, d_up, d_out, d_head, d_gain, d_bias, loss = unpack_call(core, mine, other)
    return (
        out4.reshape(pair.shape),
        loss.reshape(()),
        d_gain.reshape(width),
        d_bias.reshape(width),
        d_gate,
        d_up,
        d_out,
        d_head.T,
    )


def solution(mesh):
    placed = (
        P("row", "col", None),
        P(),
        P(),
        P(),
        P(),
        P(),
        P(),
        P(AXES, None),
        P(AXES, None),
    )
    return jax.shard_map(
        shards,
        mesh=mesh,
        in_specs=placed,
        out_specs=(P("row", "col", None), P(), P(), P(), P(), P(), P(), P()),
        check_vma=False,
    )
```
